256 devices in a mesh: ctx: 32 (over x, z), head: 8 (over y, core).
Axes of the slice: x: 4, y: 4, z: 8, core: 2. Of those that a mesh axis runs over, the one named last changes fastest.
Arguments:
- ssm_input: bfloat16 [8192, 8192], P('ctx', 'head'), may hold values from -32 to 32
- gate_input: bfloat16 [8192, 8192], P('ctx', 'head'), may hold values from -6 to 6
- write_map: bfloat16 [8192, 128], P('ctx'), may hold values from -0.5 to 0.5
- read_map: bfloat16 [8192, 128], P('ctx'), may hold values from -0.5 to 0.5
- log_decay: float32 [8192, 64], P('ctx', 'head'), may hold values from -2.2 to 0
- doc_start: int32 [8192], P('ctx'), may hold values from 0 to 8064, as said below
- ssm_grad: bfloat16 [8192, 8192], P('ctx', 'head'), may hold values from -6 to 6
- att_queries: bfloat16 [8192, 4096], P('ctx', 'head'), may hold values from -32 to 32
- att_keys: bfloat16 [8192, 4096], P('ctx', 'head'), may hold values from -20 to 20
- att_values: bfloat16 [8192, 4096], P('ctx', 'head'), may hold values from -6 to 6
- att_grad: bfloat16 [8192, 4096], P('ctx', 'head'), may hold values from -6 to 6
Outputs:
- mixer_out: bfloat16 [8192, 8192], P('ctx', 'head')
- window_out: bfloat16 [8192, 4096], P('ctx', 'head')
- input_grad: bfloat16 [8192, 8192], P('ctx', 'head')
- gate_grad: bfloat16 [8192, 8192], P('ctx', 'head')
- write_grad: bfloat16 [8192, 128], P('ctx')
- read_grad: bfloat16 [8192, 128], P('ctx')
- query_grad: bfloat16 [8192, 4096], P('ctx', 'head')
- key_grad: bfloat16 [8192, 4096], P('ctx', 'head')
- value_grad: bfloat16 [8192, 4096], P('ctx', 'head')
The draws below stay inside these ranges and needn't reach their ends.
Inputs may be any that keep to these rules, and one draw needn't show every extreme that they name: doc_start[t] is the position of the first token of the document holding token t; the 8 documents are runs of consecutive positions, the first starts at 0 and the last at 8064; one document other than the first and the last is exactly 4608 tokens long.
All inputs are finite; a program needn't handle non-finite values.
Results may differ from the reference program's by a relative error of at most 0.007.
Values may be sent and summed in bfloat16 or wider, within the bound.
A program may use at most 128 MiB of HBM per device.

```python
import math
import jax
import jax.numpy as jnp
from jax import lax

SSM_HEADS = 64
HEAD_DIM = 128
STATE = 128
ATT_HEADS = 32
ATT_DIM = 128
WINDOW = 4096
BLOCK = 128
TOK_DEV = 256
DOCS = 8
TOKENS = 8192


def draw_ssm_input(key, part):
    width_all = SSM_HEADS * HEAD_DIM
    first_key, second_key = jax.random.split(key, 2)
    column_head = (jnp.arange(width_all) // HEAD_DIM).astype(jnp.float32)
    ramp = jnp.exp(math.log(3.0) * column_head / (SSM_HEADS - 1))
    jitter = jnp.exp(jax.random.uniform(second_key, (width_all,), minval=-0.4, maxval=0.4))
    base = jnp.clip(jax.random.normal(first_key, (TOKENS, width_all)), -3.5, 3.5)
    return (base * ramp[None, :] * jitter[None, :]).astype(jnp.bfloat16)


def draw_log_decay(key, part):
    subkeys = jax.random.split(key, 6)
    share = 0.5
    slow = jax.random.uniform(subkeys[0], (SSM_HEADS,)) < share
    slow_rate = jax.random.uniform(subkeys[1], (SSM_HEADS,), minval=0.2, maxval=0.6) / TOKENS
    fast_rate = 1.0 / jax.random.uniform(subkeys[2], (SSM_HEADS,), minval=30.0, maxval=50.0)
    base_rate = jnp.where(slow, slow_rate, fast_rate)
    factor = jnp.exp(jax.random.uniform(subkeys[3], (TOKENS, SSM_HEADS), minval=-0.69, maxval=0.69))
    spot_locations = jax.random.randint(subkeys[4], (3, SSM_HEADS), 0, TOKENS)
    dropped_rows = jax.random.uniform(subkeys[5], (3, SSM_HEADS), minval=math.log(0.5), maxval=math.log(0.8))
    token_position = jnp.arange(TOKENS)[:, None]
    final_result = -base_rate[None, :] * factor
    for spike_value in range(3):
        final_result = final_result + jnp.where(token_position == spot_locations[spike_value][None, :], dropped_rows[spike_value][None, :], 0.0)
    return final_result.astype(jnp.float32)


def draw_doc_start(key, part):
    last_start = TOKENS - TOK_DEV // 2
    span_len = min(WINDOW + 2 * TOK_DEV, last_start - DOCS - 2)
    place_key, rest_key = jax.random.split(key)
    span_first = jax.random.randint(place_key, (), 1, last_start - span_len).astype(jnp.int32)
    free_count = last_start - span_len - 2
    chosen = jax.random.permutation(rest_key, free_count)[:DOCS - 4].astype(jnp.int32)
    others = jnp.where(chosen + 1 < span_first, chosen + 1, chosen + span_len + 2).astype(jnp.int32)
    cuts = jnp.concatenate([others, span_first.reshape(1), (span_first + span_len).reshape(1), jnp.full((1,), last_start, jnp.int32)])
    token_position = jnp.arange(TOKENS)[:, None]
    return jnp.max(jnp.where(cuts[None, :] <= token_position, cuts[None, :], 0), axis=1).astype(jnp.int32)


def attention_pair(key):
    base_key = jax.random.fold_in(key, 17)
    first_key, second_key = jax.random.split(base_key, 2)
    width_all = ATT_HEADS * ATT_DIM
    queries = jnp.clip(jax.random.normal(first_key, (TOKENS, width_all)), -6.0, 6.0)
    keys_out = 3.0 * jnp.clip(jax.random.normal(second_key, (TOKENS, width_all)), -6.0, 6.0)
    return (queries, keys_out)


def draw_att_queries(key, part):
    return attention_pair(key)[0].astype(jnp.bfloat16)


def draw_att_keys(key, part):
    return attention_pair(key)[1].astype(jnp.bfloat16)


def block_levels(rng, extent, cuts, low, largest):
    factor_of = 1.0
    for position, blocks in cuts:
        heights = jax.random.uniform(jax.random.fold_in(jax.random.fold_in(rng, 6), position), (blocks,), jnp.float32, low / len(cuts), largest / len(cuts))
        factor_of = factor_of * jnp.repeat(jnp.exp(heights), extent[position] // blocks).reshape((-1,) + (1,) * (len(extent) - 1 - position))
    return factor_of


def noise(key, extent, scale, bound, pieces=(), kind=jnp.bfloat16):
    values = scale * jax.random.normal(key, extent, jnp.float32)
    if pieces:
        values = values * block_levels(key, extent, pieces, -0.22, 0.18)
    return jnp.clip(values, -bound, bound).astype(kind)


def setup_inputs(seed: int = 0) -> dict:
    key_of = jax.random.split(jax.random.key(seed), 12)
    return {
        "ssm_input": draw_ssm_input(jax.random.fold_in(key_of[11], 71), 0),
        "gate_input": noise(key_of[1], (TOKENS, SSM_HEADS * HEAD_DIM), 1.0, 6.0, ((0, 32), (1, 8))),
        "write_map": noise(key_of[2], (TOKENS, STATE), STATE ** -0.5, 0.5, ((0, 32),)),
        "read_map": noise(key_of[3], (TOKENS, STATE), STATE ** -0.5, 0.5, ((0, 32),)),
        "log_decay": draw_log_decay(jax.random.fold_in(key_of[11], 71), 0),
        "doc_start": draw_doc_start(jax.random.fold_in(key_of[11], 71), 0),
        "ssm_grad": noise(key_of[6], (TOKENS, SSM_HEADS * HEAD_DIM), 1.0, 6.0, ((0, 32), (1, 8))),
        "att_queries": draw_att_queries(jax.random.fold_in(key_of[11], 71), 0),
        "att_keys": draw_att_keys(jax.random.fold_in(key_of[11], 71), 0),
        "att_values": noise(key_of[9], (TOKENS, ATT_HEADS * ATT_DIM), 1.0, 6.0, ((0, 32), (1, 8))),
        "att_grad": noise(key_of[10], (TOKENS, ATT_HEADS * ATT_DIM), 1.0, 6.0, ((0, 32), (1, 8))),
    }


PRECISE = lax.Precision.HIGHEST
EPSILON = 1e-05

def run_scan(keys_in, values_in, log_rates, doc_marks, query_shared, query_heads):
    total_len = keys_in.shape[0]
    block_count = total_len // BLOCK

    def split(array):
        return array.reshape((block_count, BLOCK) + array.shape[1:])
    piece_list = (split(keys_in), split(values_in), split(log_rates), split(doc_marks), split(query_shared))
    if query_heads is not None:
        piece_list = piece_list + (split(query_heads),)
    lower = jnp.arange(BLOCK)[:, None] >= jnp.arange(BLOCK)[None, :]
    head_count = values_in.shape[1]
    start_state = jnp.zeros((head_count, keys_in.shape[1], values_in.shape[2]), jnp.float32)

    def step(running, piece):
        state, prev_mark = running
        key_blk, value_blk, rate_blk, mark_blk, query_blk = piece[:5]
        cumulative = jnp.cumsum(rate_blk, axis=0)
        joined = (mark_blk[:, None] == mark_blk[None, :]) & lower
        spread = cumulative[:, None, :] - cumulative[None, :, :]
        decay = jnp.where(joined[:, :, None], jnp.exp(jnp.minimum(spread, 0.0)), 0.0)
        enter = jnp.where((mark_blk == prev_mark)[:, None], jnp.exp(cumulative), 0.0)
        scores = jnp.dot(query_blk, key_blk.T, precision=PRECISE)
        mixed = jnp.einsum('tsh,shp->thp', decay * scores[:, :, None], value_blk, precision=PRECISE)
        mixed = mixed + enter[:, :, None] * jnp.einsum('tn,hnp->thp', query_blk, state, precision=PRECISE)
        results = (mixed,)
        if len(piece) > 5:
            head_query = piece[5]
            inner = jnp.einsum('thp,shp->tsh', head_query, value_blk, precision=PRECISE)
            shared = jnp.einsum('tsh,sn->tn', decay * inner, key_blk, precision=PRECISE)
            shared = shared + jnp.einsum('th,thp,hnp->tn', enter, head_query, state, precision=PRECISE)
            results = results + (shared,)
        to_end = jnp.where((mark_blk == mark_blk[-1])[:, None], jnp.exp(cumulative[-1:] - cumulative), 0.0)
        keep = jnp.where(mark_blk[-1] == prev_mark, jnp.exp(cumulative[-1]), 0.0)
        new_state = keep[:, None, None] * state + jnp.einsum('sh,sn,shp->hnp', to_end, key_blk, value_blk, precision=PRECISE)
        return ((new_state, mark_blk[-1]), results)
    start = (start_state, jnp.array(-1.0, jnp.float32))
    _, results = lax.scan(step, start, piece_list)
    mixed = results[0].reshape((total_len,) + values_in.shape[1:])
    if query_heads is not None:
        return (mixed, results[1].reshape(total_len, keys_in.shape[1]))
    return (mixed, None)

def attend(head_index, queries, keys_in, values_in, grads_in, doc_start):
    query_head = lax.dynamic_slice_in_dim(queries, head_index * ATT_DIM, ATT_DIM, 1)
    key_head = lax.dynamic_slice_in_dim(keys_in, head_index * ATT_DIM, ATT_DIM, 1)
    value_head = lax.dynamic_slice_in_dim(values_in, head_index * ATT_DIM, ATT_DIM, 1)
    grad_head = lax.dynamic_slice_in_dim(grads_in, head_index * ATT_DIM, ATT_DIM, 1)
    pad_rows = jnp.zeros((WINDOW, ATT_DIM), key_head.dtype)
    key_pad = jnp.concatenate([pad_rows, key_head], axis=0)
    value_pad = jnp.concatenate([pad_rows, value_head], axis=0)
    width_span = WINDOW + TOK_DEV
    score_scale = ATT_DIM ** (-0.5)
    block_count = TOKENS // TOK_DEV

    def step(running, block_index):
        key_acc, value_acc = running
        first = block_index * TOK_DEV
        query_blk = lax.dynamic_slice_in_dim(query_head, first, TOK_DEV, 0)
        grad_blk = lax.dynamic_slice_in_dim(grad_head, first, TOK_DEV, 0)
        start_blk = lax.dynamic_slice_in_dim(doc_start, first, TOK_DEV, 0)
        key_blk = lax.dynamic_slice_in_dim(key_pad, first, width_span, 0)
        value_blk = lax.dynamic_slice_in_dim(value_pad, first, width_span, 0)
        query_pos = first + jnp.arange(TOK_DEV, dtype=jnp.int32)
        key_pos = first - WINDOW + jnp.arange(width_span, dtype=jnp.int32)
        visible = (key_pos[None, :] <= query_pos[:, None]) & (query_pos[:, None] - key_pos[None, :] < WINDOW) & (key_pos[None, :] >= start_blk[:, None])
        score = jnp.dot(query_blk, key_blk.T, preferred_element_type=jnp.float32) * score_scale
        row_max = lax.optimization_barrier(jnp.max(jnp.where(visible, score, -jnp.inf), axis=1))
        expo = jnp.where(visible, jnp.exp(score - row_max[:, None]), 0.0)
        row_total = lax.optimization_barrier(jnp.sum(expo, axis=1))
        probs = expo / row_total[:, None]
        weights = probs.astype(jnp.bfloat16)
        attended = jnp.dot(weights, value_blk, preferred_element_type=jnp.float32)
        delta = lax.optimization_barrier(jnp.sum(grad_blk.astype(jnp.float32) * attended, axis=1))
        dprobs = jnp.dot(grad_blk, value_blk.T, preferred_element_type=jnp.float32)
        dscore = (probs * (dprobs - delta[:, None]) * score_scale).astype(jnp.bfloat16)
        query_grad = jnp.dot(dscore, key_blk, preferred_element_type=jnp.float32)
        key_part = jnp.dot(dscore.T, query_blk, preferred_element_type=jnp.float32)
        value_part = jnp.dot(weights.T, grad_blk, preferred_element_type=jnp.float32)
        key_acc = lax.dynamic_update_slice_in_dim(key_acc, lax.dynamic_slice_in_dim(key_acc, first, width_span, 0) + key_part, first, 0)
        value_acc = lax.dynamic_update_slice_in_dim(value_acc, lax.dynamic_slice_in_dim(value_acc, first, width_span, 0) + value_part, first, 0)
        return ((key_acc, value_acc), (attended.astype(jnp.bfloat16), query_grad.astype(jnp.bfloat16)))
    zeros_acc = jnp.zeros((WINDOW + TOKENS, ATT_DIM), jnp.float32)
    (key_acc, value_acc), (outputs, query_grads) = lax.scan(step, (zeros_acc, zeros_acc), jnp.arange(block_count, dtype=jnp.int32))
    return (outputs.reshape(TOKENS, ATT_DIM), query_grads.reshape(TOKENS, ATT_DIM), key_acc[WINDOW:].astype(jnp.bfloat16), value_acc[WINDOW:].astype(jnp.bfloat16))

def merge_heads(stacked):
    return jnp.transpose(stacked, (1, 0, 2)).reshape(TOKENS, -1)

def reference(ssm_input, gate_input, write_map, read_map, log_decay, doc_start, ssm_grad, att_queries, att_keys, att_values, att_grad):
    inputs_full = ssm_input.astype(jnp.float32).reshape(TOKENS, SSM_HEADS, HEAD_DIM)
    writes = write_map.astype(jnp.float32)
    reads = read_map.astype(jnp.float32)
    doc_marks = doc_start.astype(jnp.float32)
    mixed, _ = run_scan(writes, inputs_full, log_decay, doc_marks, reads, None)
    mixed = mixed.reshape(TOKENS, SSM_HEADS * HEAD_DIM)
    gate_full = gate_input.astype(jnp.float32)
    sigma = jax.nn.sigmoid(gate_full)
    swish = gate_full * sigma
    gated = mixed * swish
    width_all = SSM_HEADS * HEAD_DIM
    row_scale = lax.rsqrt(lax.optimization_barrier(jnp.sum(gated * gated, axis=1)) / width_all + EPSILON)
    mixer_out = (gated * row_scale[:, None]).astype(jnp.bfloat16)
    grad_full = ssm_grad.astype(jnp.float32)
    inner = lax.optimization_barrier(jnp.sum(grad_full * gated, axis=1))
    dgated = row_scale[:, None] * grad_full - (row_scale ** 3 * inner / width_all)[:, None] * gated
    dmixed = dgated * swish
    gate_grad = (dgated * mixed * sigma * (1.0 + gate_full * (1.0 - sigma))).astype(jnp.bfloat16)
    dmixed_heads = dmixed.reshape(TOKENS, SSM_HEADS, HEAD_DIM)
    _, read_sum = run_scan(writes, inputs_full, log_decay, doc_marks, reads, dmixed_heads)
    rev_rates = jnp.concatenate([jnp.zeros((1, SSM_HEADS), jnp.float32), log_decay[::-1][:-1]], axis=0)
    back, write_sum = run_scan(reads[::-1], dmixed_heads[::-1], rev_rates, doc_marks[::-1], writes[::-1], inputs_full[::-1])
    input_grad = back[::-1].reshape(TOKENS, SSM_HEADS * HEAD_DIM).astype(jnp.bfloat16)
    write_grad = write_sum[::-1].astype(jnp.bfloat16)
    read_grad = read_sum.astype(jnp.bfloat16)

    def one_head(head_index):
        return attend(head_index, att_queries, att_keys, att_values, att_grad, doc_start)
    outs, query_grads, key_grads, value_grads = lax.map(one_head, jnp.arange(ATT_HEADS, dtype=jnp.int32))
    return (mixer_out, merge_heads(outs), input_grad, gate_grad, write_grad, read_grad, merge_heads(query_grads), merge_heads(key_grads), merge_heads(value_grads))
```

```python
import functools
import math

import jax
import jax.numpy as jnp
from jax import lax
from jax.experimental import pallas as pl
from jax.experimental.pallas import tpu as pltpu
from jax.sharding import PartitionSpec as P

DIM = 128
WINDOW = 4096
EPSILON = 1e-05
ROW = 8
QUAD = 4
TQ = 256
TK = 512
HIDDEN = -1e30
F32 = jnp.float32
BF16 = jnp.bfloat16
EXACT = lax.Precision.HIGHEST
SCALE = DIM**-0.5
SCALE2 = SCALE * math.log2(math.e)
VMEM_LIMIT = 60 * 2**20


def dot(a, b, precision=None):
    return jnp.dot(a, b, preferred_element_type=F32, precision=precision)


def dot_nt(a, b):
    return lax.dot_general(a, b, (((1,), (1,)), ((), ())), preferred_element_type=F32)


def dot_tn(a, b):
    return lax.dot_general(a, b, (((0,), (0,)), ((), ())), preferred_element_type=F32)


def call(kernel, outs, *args, flops, smem=0, scratch=()):
    specs = [pl.BlockSpec(memory_space=pltpu.SMEM)] * smem
    specs += [pl.BlockSpec(memory_space=pltpu.VMEM)] * (len(args) - smem)
    moved = sum(math.prod(a.shape) * a.dtype.itemsize for a in (*args, *outs))
    return pl.pallas_call(
        kernel,
        out_shape=outs,
        in_specs=specs,
        out_specs=tuple(pl.BlockSpec(memory_space=pltpu.VMEM) for _ in outs),
        scratch_shapes=list(scratch),
        compiler_params=pltpu.CompilerParams(vmem_limit_bytes=VMEM_LIMIT),
        cost_estimate=pl.CostEstimate(flops=flops, bytes_accessed=moved, transcendentals=0),
    )(*args)


def shape(dims, dtype):
    return jax.ShapeDtypeStruct(dims, dtype)


def attention_kernel(edge_ref, bound_ref, qg_ref, kv_ref, og_ref, dkv_ref, kvt, acc):
    step = pl.program_id(0)
    keys = kv_ref.shape[0]

    @pl.when(step == 0)
    def _():
        acc[...] = jnp.zeros_like(acc)

        @pl.loop(0, keys // TK)
        def _(t):
            rows = pl.ds(pl.multiple_of(t * TK, TK), TK)
            kvt[:, rows] = kv_ref[rows, :].T

    lo_first, lo_last = edge_ref[3 * step], edge_ref[3 * step + 1]
    hi_first = edge_ref[3 * step + 2]
    hi_last = hi_first + TQ - 1
    first = lo_first // TK
    last = hi_last // TK + 1
    open_first = jnp.clip((lo_last + TK - 1) // TK, first, last)
    open_last = jnp.clip((hi_first + 1) // TK, open_first, last)

    lo, hi = bound_ref[0:1, :], bound_ref[1:2, :]
    q, g = qg_ref[:, :DIM], qg_ref[:, DIM:]
    qt, gt = q.T, g.T

    def scores(t, masked):
        rows = pl.ds(pl.multiple_of(t * TK, TK), TK)
        s = dot(kv_ref[rows, :DIM], qt)
        if masked:
            at = t * TK + lax.broadcasted_iota(jnp.int32, (TK, TQ), 0)
            s = jnp.where((at >= lo) & (at <= hi), s, HIDDEN)
        return rows, s

    def forward(masked, t, state):
        top, total, out = state
        rows, s = scores(t, masked)
        new = jnp.maximum(top, jnp.max(s, axis=0, keepdims=True))
        p = jnp.exp2((s - new) * SCALE2)
        keep = jnp.exp2((top - new) * SCALE2)
        total = total * keep + jnp.sum(p, axis=0, keepdims=True)
        out = out * keep + dot(kvt[DIM:, rows], p.astype(BF16))
        return new, total, out

    def segments(one, state):
        state = lax.fori_loop(first, open_first, functools.partial(one, True), state)
        state = lax.fori_loop(open_first, open_last, functools.partial(one, False), state)
        return lax.fori_loop(open_last, last, functools.partial(one, True), state)

    top, total, out = segments(
        forward,
        (
            jnp.full((1, TQ), HIDDEN, F32),
            jnp.zeros((1, TQ), F32),
            jnp.zeros((DIM, TQ), F32),
        ),
    )
    out = out / total
    delta = jnp.sum(gt.astype(F32) * out, axis=0, keepdims=True)
    level = top * SCALE2 + jnp.log2(total)

    def backward(masked, t, dqt):
        rows, s = scores(t, masked)
        p = jnp.exp2(s * SCALE2 - level)
        dp = dot(kv_ref[rows, DIM:], gt)
        ds = (p * (dp - delta) * SCALE).astype(BF16)
        acc[rows, :DIM] += dot(ds, q)
        acc[rows, DIM:] += dot(p.astype(BF16), g)
        return dqt + dot(kvt[:DIM, rows], ds)

    dqt = segments(backward, jnp.zeros((DIM, TQ), F32))
    og_ref[:, :DIM] = out.T.astype(BF16)
    og_ref[:, DIM:] = dqt.T.astype(BF16)

    @pl.when(step == pl.num_programs(0) - 1)
    def _():
        @pl.loop(0, keys // TK)
        def _(t):
            rows = pl.ds(pl.multiple_of(t * TK, TK), TK)
            dkv_ref[rows, :] = acc[rows, :].astype(BF16)


def attention(edges, bounds, qg, kv):
    queries, keys = qg.shape[0], kv.shape[0]
    return pl.pallas_call(
        attention_kernel,
        out_shape=(shape((queries, 2 * DIM), BF16), shape((keys, 2 * DIM), BF16)),
        grid=(queries // TQ,),
        in_specs=[
            pl.BlockSpec(memory_space=pltpu.SMEM),
            pl.BlockSpec((2, TQ), lambda i: (0, i)),
            pl.BlockSpec((TQ, 2 * DIM), lambda i: (i, 0)),
            pl.BlockSpec((keys, 2 * DIM), lambda i: (0, 0), pipeline_mode=pl.Buffered(1)),
        ],
        out_specs=(
            pl.BlockSpec((TQ, 2 * DIM), lambda i: (i, 0)),
            pl.BlockSpec((keys, 2 * DIM), lambda i: (0, 0), pipeline_mode=pl.Buffered(1)),
        ),
        scratch_shapes=[
            pltpu.VMEM((2 * DIM, keys), BF16),
            pltpu.VMEM((keys, 2 * DIM), F32),
        ],
        compiler_params=pltpu.CompilerParams(
            dimension_semantics=("arbitrary",), vmem_limit_bytes=VMEM_LIMIT
        ),
        cost_estimate=pl.CostEstimate(
            flops=14 * queries * 4096 * DIM, bytes_accessed=4 * keys * DIM * 4, transcendentals=0
        ),
    )(edges, bounds, qg, kv)


def cumulate_kernel(rate_ref, rate_t_ref, doc_ref, x_ref, write_ref, cum_ref, cum_t_ref, state_ref):
    length, heads = rate_ref.shape
    row = lax.broadcasted_iota(jnp.int32, (length, length), 0)
    col = lax.broadcasted_iota(jnp.int32, (length, length), 1)
    cum = dot((row >= col).astype(F32), rate_ref[...], EXACT)
    cum_ref[...] = cum
    cum_t_ref[...] = dot(rate_t_ref[...], (row <= col).astype(F32), EXACT)
    tail = tail_decay(cum, doc_ref[...])
    write = write_ref[...]
    for h in range(heads):
        cols = slice(h * DIM, (h + 1) * DIM)
        scaled = (x_ref[:, cols].astype(F32) * tail[:, h : h + 1]).astype(BF16)
        state_ref[h] = dot_tn(write, scaled).astype(BF16)


def tail_decay(cum, doc):
    length = cum.shape[0]
    same = doc == doc[length - 1 : length, :]
    return jnp.where(same, jnp.exp(cum[length - 1 : length, :] - cum), 0.0)


def head_decay(cum, cum_t, seen, h):
    return jnp.exp(jnp.where(seen, cum[:, h : h + 1] - cum_t[h : h + 1, :], HIDDEN))


def visible(doc, start):
    length = doc.shape[0]
    row = lax.broadcasted_iota(jnp.int32, (length, length), 0)
    col = lax.broadcasted_iota(jnp.int32, (length, length), 1)
    return (row >= col) & (start + col >= doc)


def local_kernel(at_ref, cum_ref, cum_t_ref, doc_ref, x_ref, read_ref, write_ref, mixed_ref):
    cum, cum_t = cum_ref[...], cum_t_ref[...]
    seen = visible(doc_ref[...], at_ref[0])
    scores = dot_nt(read_ref[...], write_ref[...])
    for h in range(cum.shape[1]):
        cols = slice(h * DIM, (h + 1) * DIM)
        mix = (head_decay(cum, cum_t, seen, h) * scores).astype(BF16)
        mixed_ref[:, cols] = dot(mix, x_ref[:, cols])


def link_kernel(transposed, total_ref, doc_ref, part_ref, out_ref):
    n = part_ref.shape[0]
    row = lax.broadcasted_iota(jnp.int32, (n, n), 0)
    col = lax.broadcasted_iota(jnp.int32, (n, n), 1)
    late, early = (col, row) if transposed else (row, col)
    spread = jnp.zeros((n, n), F32)
    mark = jnp.zeros((n, n), jnp.int32)
    for k in range(n):
        spread += jnp.where((early < k) & (k < late), total_ref[k], 0.0)
        mark = jnp.where(late == k + 1, doc_ref[k], mark)
    joined = (late > early) & (mark < TQ * (early + 1))
    weight = jnp.exp(jnp.where(joined, spread, HIDDEN))
    out_ref[...] = dot(weight, part_ref[...].astype(F32), EXACT).astype(BF16)


def gate_terms(gate):
    sigma = jax.nn.sigmoid(gate)
    return sigma, gate * sigma


def mix_kernel(at_ref, cum_ref, doc_ref, local_ref, read_ref, prior_ref, gate_ref, grad_ref, mixed_ref, sums_ref):
    enter = jnp.where(doc_ref[...] < at_ref[0], jnp.exp(cum_ref[...]), 0.0)
    read = read_ref[...]
    length = read.shape[0]
    squares = jnp.zeros((length, 1), F32)
    inner = jnp.zeros((length, 1), F32)
    for h in range(enter.shape[1]):
        cols = slice(h * DIM, (h + 1) * DIM)
        mixed = local_ref[:, cols] + enter[:, h : h + 1] * dot(read, prior_ref[h])
        mixed_ref[:, cols] = mixed
        gated = mixed * gate_terms(gate_ref[:, cols].astype(F32))[1]
        squares += jnp.sum(gated * gated, axis=1, keepdims=True)
        inner += jnp.sum(grad_ref[:, cols].astype(F32) * gated, axis=1, keepdims=True)
    sums_ref[:, 0:1] = squares
    sums_ref[:, 1:2] = inner


def norm_kernel(width, at_ref, cum_ref, doc_ref, sums_ref, mixed_ref, read_ref, gate_ref, grad_ref,
                out_ref, gate_grad_ref, dmixed_ref, state_ref):
    enter = jnp.where(doc_ref[...] < at_ref[0], jnp.exp(cum_ref[...]), 0.0)
    rms = lax.rsqrt(sums_ref[:, 0:1] / width + EPSILON)
    pull = rms * rms * rms * sums_ref[:, 1:2] / width
    read = read_ref[...]
    for h in range(enter.shape[1]):
        cols = slice(h * DIM, (h + 1) * DIM)
        mixed = mixed_ref[:, cols]
        gate = gate_ref[:, cols].astype(F32)
        sigma, swish = gate_terms(gate)
        gated = mixed * swish
        out_ref[:, cols] = (gated * rms).astype(BF16)
        dgated = rms * grad_ref[:, cols].astype(F32) - pull * gated
        dmixed = dgated * swish
        dmixed_ref[:, cols] = dmixed.astype(BF16)
        gate_grad_ref[:, cols] = (dgated * mixed * sigma * (1.0 + gate * (1.0 - sigma))).astype(BF16)
        state_ref[h] = dot_tn(read, (enter[:, h : h + 1] * dmixed).astype(BF16)).astype(BF16)


def adjoint_kernel(at_ref, cum_ref, cum_t_ref, doc_ref, x_ref, dmixed_ref, read_ref, write_ref, prior_ref,
                   input_ref, maps_ref):
    cum, cum_t = cum_ref[...], cum_t_ref[...]
    doc = doc_ref[...]
    seen = visible(doc, at_ref[0])
    enter = jnp.where(doc < at_ref[0], jnp.exp(cum), 0.0)
    read, write = read_ref[...], write_ref[...]
    scores = dot_nt(read, write)
    pairs = jnp.zeros_like(scores)
    read_part = jnp.zeros(read.shape, F32)
    for h in range(cum.shape[1]):
        cols = slice(h * DIM, (h + 1) * DIM)
        decay = head_decay(cum, cum_t, seen, h)
        dmixed = dmixed_ref[:, cols]
        input_ref[:, cols] = dot_tn((decay * scores).astype(BF16), dmixed)
        pairs += decay * dot_nt(dmixed, x_ref[:, cols])
        entered = (enter[:, h : h + 1] * dmixed.astype(F32)).astype(BF16)
        read_part += dot_nt(entered, prior_ref[h])
    pairs = pairs.astype(BF16)
    maps_ref[:, :DIM] = dot_tn(pairs, read)
    maps_ref[:, DIM:] = read_part + dot(pairs, write)


def finish_kernel(cum_ref, doc_ref, x_ref, write_ref, after_ref, input_ref, maps_ref, input_grad_ref, out_ref):
    tail = tail_decay(cum_ref[...], doc_ref[...])
    write = write_ref[...]
    write_part = maps_ref[:, :DIM]
    for h in range(tail.shape[1]):
        cols = slice(h * DIM, (h + 1) * DIM)
        t = tail[:, h : h + 1]
        after = after_ref[h]
        input_grad_ref[:, cols] = (input_ref[:, cols] + t * dot(write, after)).astype(BF16)
        write_part += dot_nt((x_ref[:, cols].astype(F32) * t).astype(BF16), after)
    out_ref[:, :DIM] = write_part
    out_ref[:, DIM:] = maps_ref[:, DIM:]


def by_head(a, b):
    length, width = a.shape
    both = [t.reshape(length, width // DIM, DIM).transpose(1, 0, 2) for t in (a, b)]
    return jnp.concatenate(both, axis=2)


def by_token(pair, half):
    part = pair[:, :, half * DIM : (half + 1) * DIM]
    return part.transpose(1, 0, 2).reshape(part.shape[1], -1)


def body(
    ssm_input,
    gate_input,
    write_map,
    read_map,
    log_decay,
    doc_start,
    ssm_grad,
    att_queries,
    att_keys,
    att_values,
    att_grad,
):
    n = lax.axis_size("ctx")
    me = lax.axis_index("ctx")
    length, width = ssm_input.shape
    heads = width // DIM
    width_all = width * lax.axis_size("head")
    rows = [list(range(i, i + ROW)) for i in range(0, n, ROW)]
    quads = [list(range(i, i + QUAD)) for i in range(0, n, QUAD)]

    facts = jnp.concatenate([doc_start.astype(F32), jnp.sum(log_decay, axis=0)])
    facts = lax.all_gather(facts, "ctx")
    doc_all = facts[:, :length].astype(jnp.int32)
    total_all = facts[:, length:]
    share = n // heads
    totals = lax.dynamic_index_in_dim(total_all, me // share, 1, False)
    last_doc = doc_all[:, length - 1]

    start = (me * length).astype(jnp.int32).reshape(1)
    doc_col = doc_start.reshape(length, 1)
    cum, cum_t, state = call(
        cumulate_kernel,
        (shape((length, heads), F32), shape((heads, length), F32), shape((heads, DIM, DIM), BF16)),
        log_decay, log_decay.T, doc_col, ssm_input, write_map,
        flops=2 * length * DIM * width,
    )

    def exchange(state, transposed):
        parts = lax.all_to_all(state.reshape(n, -1), "ctx", 0, 0)
        (linked,) = call(
            functools.partial(link_kernel, transposed),
            (shape(parts.shape, BF16),),
            totals, last_doc, parts,
            flops=12 * n * n * parts.shape[1], smem=2,
        )
        return lax.all_to_all(linked, "ctx", 0, 0).reshape(heads, DIM, DIM)

    kv = by_head(att_keys, att_values)
    kv_row = lax.all_to_all(jnp.concatenate([kv, kv], axis=0), "ctx", 0, 0, axis_index_groups=rows)
    kv_row = kv_row.reshape(ROW * length, 2 * DIM)
    qg = lax.all_to_all(by_head(att_queries, att_grad), "ctx", 0, 0, axis_index_groups=quads)
    qg = qg.reshape(QUAD * length, 2 * DIM)

    def rotate(a, by):
        return lax.ppermute(a, "ctx", [(i, (i + by) % n) for i in range(n)])

    kv_all = jnp.concatenate([rotate(kv_row, 2 * ROW), rotate(kv_row, ROW), kv_row], axis=0)

    prior = exchange(state, False)
    (local,) = call(
        local_kernel,
        (shape((length, width), F32),),
        start, cum, cum_t, doc_col, ssm_input, read_map, write_map,
        flops=2 * length * length * width, smem=1,
    )
    mixed, sums = call(
        mix_kernel,
        (shape((length, width), F32), shape((length, 2), F32)),
        start, cum, doc_col, local, read_map, prior, gate_input, ssm_grad,
        flops=2 * length * DIM * width, smem=1,
    )
    sums = lax.psum(sums.T, "head").T
    mixer_out, gate_grad, dmixed, back = call(
        functools.partial(norm_kernel, width_all),
        (shape((length, width), BF16), shape((length, width), BF16), shape((length, width), BF16),
         shape((heads, DIM, DIM), BF16)),
        start, cum, doc_col, sums, mixed, read_map, gate_input, ssm_grad,
        flops=2 * length * DIM * width, smem=1,
    )
    after = exchange(back, True)
    input_part, maps_part = call(
        adjoint_kernel,
        (shape((length, width), F32), shape((length, 2 * DIM), F32)),
        start, cum, cum_t, doc_col, ssm_input, dmixed, read_map, write_map, prior,
        flops=6 * length * length * width, smem=1,
    )

    quad = me // QUAD
    count = QUAD * length
    base = (me // ROW - 2) * (ROW * length)
    docs = lax.dynamic_slice_in_dim(doc_all.reshape(-1), quad * count, count)
    high = 2 * ROW * length + (quad % 2) * count + jnp.arange(count, dtype=jnp.int32)
    low = jnp.maximum(docs - base, high - (WINDOW - 1))
    tiles = count // TQ
    edges = jnp.stack([low[::TQ], low[TQ - 1 :: TQ], high[::TQ]], axis=1).reshape(3 * tiles)
    og, dkv = attention(edges, jnp.stack([low, high]), qg, kv_all)
    og = lax.all_to_all(og.reshape(QUAD, length, 2 * DIM), "ctx", 0, 0, axis_index_groups=quads)
    dkv = dkv.reshape(3, ROW * length, 2 * DIM)
    dkv_sum = (
        dkv[2].astype(F32)
        + rotate(dkv[1], -ROW).astype(F32)
        + rotate(dkv[0], -2 * ROW).astype(F32)
    ).astype(BF16)
    dkv_sum = lax.all_to_all(dkv_sum.reshape(ROW, length, 2 * DIM), "ctx", 0, 0, axis_index_groups=rows)
    dkv_sum = (dkv_sum[:QUAD].astype(F32) + dkv_sum[QUAD:].astype(F32)).astype(BF16)

    input_grad, maps = call(
        finish_kernel,
        (shape((length, width), BF16), shape((length, 2 * DIM), F32)),
        cum, doc_col, ssm_input, write_map, after, input_part, maps_part,
        flops=4 * length * DIM * width,
    )
    maps = lax.psum(maps, "head").astype(BF16)
    return (
        mixer_out,
        by_token(og, 0),
        input_grad,
        gate_grad,
        maps[:, :DIM],
        maps[:, DIM:],
        by_token(og, 1),
        by_token(dkv_sum, 0),
        by_token(dkv_sum, 1),
    )


def solution(mesh):
    tokens, both = P("ctx", None), P("ctx", "head")
    in_specs = (both, both, tokens, tokens, both, P("ctx"), both, both, both, both, both)
    out_specs = (both, both, both, both, tokens, tokens, both, both, both)
    return jax.shard_map(body, mesh=mesh, in_specs=in_specs, out_specs=out_specs, check_vma=False)
```

```python
import functools
import math

import jax
import jax.numpy as jnp
from jax import lax
from jax.experimental import pallas as pl
from jax.experimental.pallas import tpu as pltpu
from jax.sharding import PartitionSpec as P

DIM = 128
WINDOW = 4096
EPSILON = 1e-05
ROW = 8
QUAD = 4
TQ = 256
TK = 512
HIDDEN = -1e30
F32 = jnp.float32
BF16 = jnp.bfloat16
EXACT = lax.Precision.HIGHEST
SCALE = DIM**-0.5
SCALE2 = SCALE * math.log2(math.e)
VMEM_LIMIT = 60 * 2**20
MESH = pl.DeviceIdType.MESH
TOK = 256
SPAN = ROW * TOK


def dot(a, b, precision=None):
    return jnp.dot(a, b, preferred_element_type=F32, precision=precision)


def dot_nt(a, b):
    return lax.dot_general(a, b, (((1,), (1,)), ((), ())), preferred_element_type=F32)


def dot_tn(a, b):
    return lax.dot_general(a, b, (((0,), (0,)), ((), ())), preferred_element_type=F32)


def shape(dims, dtype):
    return jax.ShapeDtypeStruct(dims, dtype)


def attention_kernel(facts_ref, qg_ref, kv_ref, og_ref, dkv_ref, kvt, acc):
    step = pl.program_id(0)
    me = lax.axis_index("ctx")
    quad = me // QUAD
    keys = kv_ref.shape[0]

    @pl.when(step == 0)
    def _():
        acc[...] = jnp.zeros_like(acc)

        @pl.loop(0, keys // TK)
        def _(t):
            rows = pl.ds(pl.multiple_of(t * TK, TK), TK)
            kvt[:, rows] = kv_ref[rows, :].T

    docs = facts_ref[quad * QUAD + step]
    docs = jnp.concatenate([docs[0:1, :], docs[1:2, :]], axis=1).astype(jnp.int32)
    hi_first = 2 * SPAN + (quad % 2) * (QUAD * TOK) + step * TQ
    hi_last = hi_first + TQ - 1
    hi = hi_first + lax.broadcasted_iota(jnp.int32, (1, TQ), 1)
    lo = jnp.maximum(docs - (me // ROW - 2) * SPAN, hi - (WINDOW - 1))
    lo_first, lo_last = jnp.min(lo), jnp.max(lo)
    first = lo_first // TK
    last = hi_last // TK + 1
    open_first = jnp.clip((lo_last + TK - 1) // TK, first, last)
    open_last = jnp.clip((hi_first + 1) // TK, open_first, last)

    q, g = qg_ref[:, :DIM], qg_ref[:, DIM:]
    qt, gt = q.T, g.T

    def scores(t, masked):
        rows = pl.ds(pl.multiple_of(t * TK, TK), TK)
        s = dot(kv_ref[rows, :DIM], qt)
        if masked:
            at = t * TK + lax.broadcasted_iota(jnp.int32, (TK, TQ), 0)
            s = jnp.where((at >= lo) & (at <= hi), s, HIDDEN)
        return rows, s

    def forward(masked, t, state):
        top, total, out = state
        rows, s = scores(t, masked)
        new = jnp.maximum(top, jnp.max(s, axis=0, keepdims=True))
        p = jnp.exp2((s - new) * SCALE2)
        keep = jnp.exp2((top - new) * SCALE2)
        total = total * keep + jnp.sum(p, axis=0, keepdims=True)
        out = out * keep + dot(kvt[DIM:, rows], p.astype(BF16))
        return new, total, out

    def segments(one, state):
        state = lax.fori_loop(first, open_first, functools.partial(one, True), state)
        state = lax.fori_loop(open_first, open_last, functools.partial(one, False), state)
        return lax.fori_loop(open_last, last, functools.partial(one, True), state)

    top, total, out = segments(
        forward,
        (
            jnp.full((1, TQ), HIDDEN, F32),
            jnp.zeros((1, TQ), F32),
            jnp.zeros((DIM, TQ), F32),
        ),
    )
    out = out / total
    delta = jnp.sum(gt.astype(F32) * out, axis=0, keepdims=True)
    level = top * SCALE2 + jnp.log2(total)

    def backward(masked, t, dqt):
        rows, s = scores(t, masked)
        p = jnp.exp2(s * SCALE2 - level)
        dp = dot(kv_ref[rows, DIM:], gt)
        ds = (p * (dp - delta) * SCALE).astype(BF16)
        acc[rows, :DIM] += dot(ds, q)
        acc[rows, DIM:] += dot(p.astype(BF16), g)
        return dqt + dot(kvt[:DIM, rows], ds)

    dqt = segments(backward, jnp.zeros((DIM, TQ), F32))
    og_ref[:, :DIM] = out.T.astype(BF16)
    og_ref[:, DIM:] = dqt.T.astype(BF16)

    @pl.when(step == pl.num_programs(0) - 1)
    def _():
        @pl.loop(0, keys // TK)
        def _(t):
            rows = pl.ds(pl.multiple_of(t * TK, TK), TK)
            dkv_ref[rows, :] = acc[rows, :].astype(BF16)


def attention(facts, qg, kv):
    queries, keys = qg.shape[0], kv.shape[0]
    return pl.pallas_call(
        attention_kernel,
        out_shape=(shape((queries, 2 * DIM), BF16), shape((keys, 2 * DIM), BF16)),
        grid=(queries // TQ,),
        in_specs=[
            pl.BlockSpec(facts.shape, lambda i: (0, 0, 0), pipeline_mode=pl.Buffered(1)),
            pl.BlockSpec((TQ, 2 * DIM), lambda i: (i, 0)),
            pl.BlockSpec((keys, 2 * DIM), lambda i: (0, 0), pipeline_mode=pl.Buffered(1)),
        ],
        out_specs=(
            pl.BlockSpec((TQ, 2 * DIM), lambda i: (i, 0)),
            pl.BlockSpec((keys, 2 * DIM), lambda i: (0, 0), pipeline_mode=pl.Buffered(1)),
        ),
        scratch_shapes=[
            pltpu.VMEM((2 * DIM, keys), BF16),
            pltpu.VMEM((keys, 2 * DIM), F32),
        ],
        compiler_params=pltpu.CompilerParams(
            dimension_semantics=("arbitrary",), vmem_limit_bytes=VMEM_LIMIT
        ),
        cost_estimate=pl.CostEstimate(
            flops=14 * queries * 4096 * DIM, bytes_accessed=4 * keys * DIM * 4, transcendentals=0
        ),
    )(facts, qg, kv)


def send(src, dst, sent, arrived, **where):
    return pltpu.make_async_remote_copy(
        src_ref=src, dst_ref=dst, send_sem=sent, recv_sem=arrived, device_id=where, device_id_type=MESH
    )


def ring(at, by, size):
    return lax.rem(at + by + size, size)


def greet():
    barrier = pltpu.get_barrier_semaphore()
    ctx, head = lax.axis_size("ctx"), lax.axis_size("head")
    for axis, size in (("ctx", ctx), ("head", head)):
        if size == 1:
            continue
        me = lax.axis_index(axis)

        @pl.loop(1, size)
        def _(d):
            pl.semaphore_signal(
                barrier, inc=1, device_id={axis: ring(me, d, size)}, device_id_type=MESH
            )

    pl.semaphore_wait(barrier, ctx + head - 2)


def scatter(axis, src, dst, sent, arrived):
    size, me = lax.axis_size(axis), lax.axis_index(axis)

    @pl.loop(1, size)
    def _(d):
        to = ring(me, d, size)
        send(src.at[to], dst.at[me], sent.at[d], arrived.at[d], **{axis: to}).start()


def spread(axis, src, dst, sent, arrived):
    size, me = lax.axis_size(axis), lax.axis_index(axis)

    @pl.loop(1, size)
    def _(d):
        send(src, dst.at[me], sent.at[d], arrived.at[d], **{axis: ring(me, d, size)}).start()


def collect(axis, dst, sent, arrived):
    size, me = lax.axis_size(axis), lax.axis_index(axis)

    @pl.loop(1, size)
    def _(d):
        block = dst.at[ring(me, -d, size)]
        send(block, block, sent.at[d], arrived.at[d], **{axis: ring(me, d, size)}).wait_recv()


def settle(axis, src, sent, arrived):
    size, me = lax.axis_size(axis), lax.axis_index(axis)

    @pl.loop(1, size)
    def _(d):
        send(src, src, sent.at[d], arrived.at[d], **{axis: ring(me, d, size)}).wait_send()


def column(row):
    n = row.shape[1]
    same = lax.broadcasted_iota(jnp.int32, (n, n), 0) == lax.broadcasted_iota(jnp.int32, (n, n), 1)
    return jnp.sum(jnp.where(same, row, 0.0), axis=1, keepdims=True)


def tail_decay(cum, doc):
    length = cum.shape[0]
    same = doc == doc[length - 1 : length, :]
    return jnp.where(same, jnp.exp(cum[length - 1 : length, :] - cum), 0.0)


def head_decay(cum, cum_t, seen, h):
    return jnp.exp(jnp.where(seen, cum[:, h : h + 1] - cum_t[h : h + 1, :], HIDDEN))


def visible(doc, start):
    length = doc.shape[0]
    row = lax.broadcasted_iota(jnp.int32, (length, length), 0)
    col = lax.broadcasted_iota(jnp.int32, (length, length), 1)
    return (row >= col) & ((start + col).astype(F32) >= doc)


def gate_terms(gate):
    sigma = jax.nn.sigmoid(gate)
    return sigma, gate * sigma


def cols_of(h):
    return slice(h * DIM, (h + 1) * DIM)


def head_state(buf, h, heads):
    share = buf.shape[0] // heads
    return buf[h * share : (h + 1) * share].reshape(DIM, DIM)


def put_state(buf, h, heads, value):
    share = buf.shape[0] // heads
    buf[h * share : (h + 1) * share] = value.astype(BF16).reshape(share, DIM // share, DIM)


def chain(parts, linked, factor, reverse):
    n = parts.shape[0]
    edge = n - 1 if reverse else 0
    linked[edge] = jnp.zeros(linked.shape[1:], BF16)

    def one(step, total):
        i = n - 1 - step if reverse else step
        total = total * factor[pl.ds(i, 1), :] + parts[i].astype(F32)
        linked[i - 1 if reverse else i + 1] = total.astype(BF16)
        return total

    lax.fori_loop(0, n - 1, one, jnp.zeros(parts.shape[1:], F32))


def forward_kernel(
    doc_ref, rate_ref, x_ref, gate_ref, grad_ref, write_ref, read_ref, q_ref, k_ref, v_ref, g_ref,
    kv_ref, qg_ref, facts_ref, factor_ref, cum_ref, cum_t_ref, doc_col_ref, prior_ref, mixed_ref, sums_ref,
    fact, wide, parts_out, parts_in, linked, sums_out, sums_in,
    kv_s, kv_r, qg_s, qg_r, one_s, one_r, two_s, two_r,
    fact_s, fact_r, part_s, part_r, link_s, link_r, sum_s, sum_r,
):
    ctx = lax.axis_size("ctx")
    me, head = lax.axis_index("ctx"), lax.axis_index("head")
    x, z = me // ROW, lax.rem(me, ROW)
    spot = lax.rem(me, QUAD)
    length, heads = rate_ref.shape
    start = me * length

    docs = doc_ref[...].astype(F32)
    fact[...] = jnp.zeros_like(fact)
    fact[0:2, :] = docs
    rate = rate_ref[...]
    fact[2:3, :heads] = jnp.sum(rate, axis=0, keepdims=True)
    facts_ref[me] = fact[...]

    greet()
    spread("ctx", fact, facts_ref, fact_s, fact_r)

    def block(ref, a):
        return ref.at[:, pl.ds(pl.multiple_of(a * DIM, DIM), DIM)]

    def rows_of(first, z_from):
        return pl.ds(pl.multiple_of(first + z_from * TOK, TOK), TOK)

    halves = (slice(0, DIM), slice(DIM, 2 * DIM))

    def key_copies(d, z_from, z_to):
        out = []
        for i, ref in enumerate((k_ref, v_ref)):
            src = block(ref, lax.rem(z_to, QUAD))
            dst = kv_ref.at[rows_of(2 * SPAN, z_from), halves[i]]
            if d == 0:
                out.append(pltpu.make_async_copy(src, dst, kv_r.at[d, i]))
            else:
                out.append(send(src, dst, kv_s.at[d, i], kv_r.at[d, i], ctx=x * ROW + z_to))
        return out

    def query_copies(d, from_, to):
        out = []
        for i, ref in enumerate((q_ref, g_ref)):
            src = block(ref, to)
            dst = qg_ref.at[rows_of(0, from_), halves[i]]
            if d == 0:
                out.append(pltpu.make_async_copy(src, dst, qg_r.at[d, i]))
            else:
                out.append(send(src, dst, qg_s.at[d, i], qg_r.at[d, i], ctx=me - spot + to))
        return out

    for d in range(ROW):
        for copy in key_copies(d, z, ring(z, d, ROW)):
            copy.start()
    for d in range(QUAD):
        for copy in query_copies(d, spot, ring(spot, d, QUAD)):
            copy.start()

    row = lax.broadcasted_iota(jnp.int32, (length, length), 0)
    col = lax.broadcasted_iota(jnp.int32, (length, length), 1)
    cum = dot((row >= col).astype(F32), rate, EXACT)
    cum_ref[...] = cum
    wide[...] = jnp.zeros_like(wide)
    wide[:, :heads] = cum
    cum_t = wide[...].T[:heads]
    cum_t_ref[...] = cum_t
    doc = jnp.concatenate([column(docs[0:1, :]), column(docs[1:2, :])], axis=0)
    doc_col_ref[...] = doc
    tail = tail_decay(cum, doc)
    write, read = write_ref[...], read_ref[...]
    for h in range(heads):
        scaled = (x_ref[:, cols_of(h)].astype(F32) * tail[:, h : h + 1]).astype(BF16)
        put_state(parts_out, h, heads, dot_tn(write, scaled))
    parts_in[me] = parts_out[me]
    scatter("ctx", parts_out, parts_in, part_s, part_r)

    seen = visible(doc, start)
    scores = dot_nt(read, write)
    for h in range(heads):
        mix = (head_decay(cum, cum_t, seen, h) * scores).astype(BF16)
        mixed_ref[:, cols_of(h)] = dot(mix, x_ref[:, cols_of(h)])

    collect("ctx", facts_ref, fact_s, fact_r)
    at = lax.broadcasted_iota(jnp.int32, (ctx, 1), 0)
    lane = lax.broadcasted_iota(jnp.int32, (ctx, DIM), 1)
    mine = me // (ctx // heads)
    total = jnp.sum(jnp.where(lane == mine, facts_ref[:, 2, :], 0.0), axis=1, keepdims=True)
    final = jnp.sum(jnp.where(lane == DIM - 1, facts_ref[:, 1, :], 0.0), axis=1, keepdims=True)
    factor = jnp.where(final < (at * length).astype(F32), jnp.exp(total), 0.0)
    factor_ref[...] = jnp.broadcast_to(factor, factor_ref.shape)

    collect("ctx", parts_in, part_s, part_r)
    chain(parts_in, linked, factor_ref, False)
    prior_ref[me] = linked[me]
    scatter("ctx", linked, prior_ref, link_s, link_r)

    def pass_on(d, first, sent, arrived):
        z_from = ring(z, -d, ROW)
        return send(
            kv_ref.at[rows_of(first, z_from), :],
            kv_ref.at[rows_of(first - SPAN, z_from), :],
            sent.at[d], arrived.at[d], ctx=lax.rem(me + ROW, ctx),
        )

    last_row = ctx // ROW - 1
    for d in range(ROW):
        for copy in key_copies(d, ring(z, -d, ROW), z):
            if d == 0:
                copy.wait()
            else:
                copy.wait_recv()

        @pl.when(x < last_row)
        def _():
            pass_on(d, 2 * SPAN, one_s, one_r).start()

    collect("ctx", prior_ref, link_s, link_r)
    enter = jnp.where(doc < start.astype(F32), jnp.exp(cum), 0.0)
    squares = jnp.zeros((length, 1), F32)
    inner = jnp.zeros((length, 1), F32)
    for h in range(heads):
        mixed = mixed_ref[:, cols_of(h)] + enter[:, h : h + 1] * dot(read, head_state(prior_ref, h, heads))
        mixed_ref[:, cols_of(h)] = mixed
        gated = mixed * gate_terms(gate_ref[:, cols_of(h)].astype(F32))[1]
        squares += jnp.sum(gated * gated, axis=1, keepdims=True)
        inner += jnp.sum(grad_ref[:, cols_of(h)].astype(F32) * gated, axis=1, keepdims=True)
    wide[:, 0:1] = squares
    wide[:, 1:2] = inner
    sums_out[...] = wide[...].T[:8]
    sums_in[head] = sums_out[...]
    spread("head", sums_out, sums_in, sum_s, sum_r)

    def wanted(d):
        return (z < QUAD) | (ring(z, -d, ROW) >= QUAD)

    for d in range(ROW):

        @pl.when(x >= 1)
        def _():
            pass_on(d, 2 * SPAN, one_s, one_r).wait_recv()

        @pl.when((x >= 1) & (x < last_row) & wanted(d))
        def _():
            pass_on(d, SPAN, two_s, two_r).start()

    collect("head", sums_in, sum_s, sum_r)
    sums = sums_in[0]
    for i in range(1, sums_in.shape[0]):
        sums += sums_in[i]
    sums_ref[...] = jnp.concatenate([sums, jnp.zeros((DIM - 8, length), F32)], axis=0).T

    for d in range(QUAD):
        for copy in query_copies(d, ring(spot, -d, QUAD), spot):
            if d == 0:
                copy.wait()
            else:
                copy.wait_recv()
    for d in range(ROW):

        @pl.when((x >= 2) & wanted(d))
        def _():
            pass_on(d, SPAN, two_s, two_r).wait_recv()

    for d in range(1, ROW):
        for copy in key_copies(d, z, ring(z, d, ROW)):
            copy.wait_send()
    for d in range(1, QUAD):
        for copy in query_copies(d, spot, ring(spot, d, QUAD)):
            copy.wait_send()
    for d in range(ROW):

        @pl.when(x < last_row)
        def _():
            pass_on(d, 2 * SPAN, one_s, one_r).wait_send()

        @pl.when((x >= 1) & (x < last_row) & wanted(d))
        def _():
            pass_on(d, SPAN, two_s, two_r).wait_send()

    settle("ctx", fact, fact_s, fact_r)
    settle("ctx", parts_out.at[0], part_s, part_r)
    settle("ctx", linked.at[0], link_s, link_r)
    settle("head", sums_out, sum_s, sum_r)


def backward_kernel(
    width, sums_ref, mixed_ref, x_ref, gate_ref, grad_ref, write_ref, read_ref, cum_ref, cum_t_ref, doc_col_ref,
    prior_ref, factor_ref, og_ref, dkv_ref,
    out_ref, window_ref, input_grad_ref, gate_grad_ref, write_grad_ref, read_grad_ref,
    query_grad_ref, key_grad_ref, value_grad_ref,
    dmixed_ref, input_ref, parts_out, parts_in, linked, after_ref, maps, maps_in, maps_sum, maps_all,
    far_in, near_out, near_in, row_out, row_in,
    og_s, og_r, far_s, far_r, near_s, near_r, row_s, row_r,
    part_s, part_r, link_s, link_r, map_s, map_r, all_s, all_r,
):
    ctx, crew = lax.axis_size("ctx"), lax.axis_size("head")
    me, head = lax.axis_index("ctx"), lax.axis_index("head")
    x, z = me // ROW, lax.rem(me, ROW)
    spot = lax.rem(me, QUAD)
    length, heads = cum_ref.shape
    start = me * length
    last_row = ctx // ROW - 1
    greet()

    def rows_of(first, z_from):
        return pl.ds(pl.multiple_of(first + z_from * TOK, TOK), TOK)

    halves = (slice(0, DIM), slice(DIM, 2 * DIM))

    def result_copies(d, a, to):
        out = []
        for i, ref in enumerate((window_ref, query_grad_ref)):
            src = og_ref.at[rows_of(0, to), halves[i]]
            dst = ref.at[:, pl.ds(pl.multiple_of(a * DIM, DIM), DIM)]
            if d == 0:
                out.append(pltpu.make_async_copy(src, dst, og_r.at[d, i]))
            else:
                out.append(send(src, dst, og_s.at[d, i], og_r.at[d, i], ctx=me - spot + to))
        return out

    def wanted(b):
        return (z < QUAD) | (b >= QUAD)

    def back(src, dst, b, sent, arrived):
        return send(src, dst, sent.at[b], arrived.at[b], ctx=lax.rem(me + ctx - ROW, ctx))

    def far(b):
        return back(dkv_ref.at[rows_of(0, b), :], far_in.at[b], b, far_s, far_r)

    def near(b):
        return back(near_out.at[b], near_in.at[b], b, near_s, near_r)

    @pl.when(x >= 2)
    def _():
        @pl.loop(0, ROW)
        def _(b):
            @pl.when(wanted(b))
            def _():
                far(b).start()

    for d in range(QUAD):
        for copy in result_copies(d, spot, ring(spot, d, QUAD)):
            copy.start()

    cum, cum_t, doc = cum_ref[...], cum_t_ref[...], doc_col_ref[...]
    enter = jnp.where(doc < start.astype(F32), jnp.exp(cum), 0.0)
    rms = lax.rsqrt(sums_ref[:, 0:1] / width + EPSILON)
    pull = rms * rms * rms * sums_ref[:, 1:2] / width
    write, read = write_ref[...], read_ref[...]
    for h in range(heads):
        cols = cols_of(h)
        mixed = mixed_ref[:, cols]
        gate = gate_ref[:, cols].astype(F32)
        sigma, swish = gate_terms(gate)
        gated = mixed * swish
        out_ref[:, cols] = (gated * rms).astype(BF16)
        dgated = rms * grad_ref[:, cols].astype(F32) - pull * gated
        dmixed = dgated * swish
        dmixed_ref[:, cols] = dmixed.astype(BF16)
        gate_grad_ref[:, cols] = (dgated * mixed * sigma * (1.0 + gate * (1.0 - sigma))).astype(BF16)
        put_state(parts_out, h, heads, dot_tn(read, (enter[:, h : h + 1] * dmixed).astype(BF16)))
    parts_in[me] = parts_out[me]
    scatter("ctx", parts_out, parts_in, part_s, part_r)

    @pl.loop(0, ROW)
    def _(b):
        own = dkv_ref[rows_of(SPAN, b), :]
        more = (x >= 1) & (x < last_row) & wanted(b)

        @pl.when(more)
        def _():
            far(b).wait_recv()
            near_out[b] = (own.astype(F32) + far_in[b].astype(F32)).astype(BF16)

        @pl.when(jnp.logical_not(more))
        def _():
            near_out[b] = own

        @pl.when(x >= 1)
        def _():
            near(b).start()

    seen = visible(doc, start)
    scores = dot_nt(read, write)
    pairs = jnp.zeros_like(scores)
    read_part = jnp.zeros(read.shape, F32)
    for h in range(heads):
        cols = cols_of(h)
        decay = head_decay(cum, cum_t, seen, h)
        dmixed = dmixed_ref[:, cols]
        input_ref[:, cols] = dot_tn((decay * scores).astype(BF16), dmixed)
        pairs += decay * dot_nt(dmixed, x_ref[:, cols])
        entered = (enter[:, h : h + 1] * dmixed.astype(F32)).astype(BF16)
        read_part += dot_nt(entered, head_state(prior_ref, h, heads))
    pairs = pairs.astype(BF16)
    write_part = dot_tn(pairs, read)
    read_part += dot(pairs, write)

    collect("ctx", parts_in, part_s, part_r)
    chain(parts_in, linked, factor_ref, True)
    after_ref[me] = linked[me]
    scatter("ctx", linked, after_ref, link_s, link_r)

    def row_copy(d, b):
        return send(row_out.at[b], row_in.at[z], row_s.at[d], row_r.at[d], ctx=x * ROW + b)

    for d in range(ROW):
        b = ring(z, d, ROW)
        own = dkv_ref[rows_of(2 * SPAN, b), :]

        @pl.when(x < last_row)
        def _():
            near(b).wait_recv()
            row_out[b] = (own.astype(F32) + near_in[b].astype(F32)).astype(BF16)

        @pl.when(x == last_row)
        def _():
            row_out[b] = own

        if d:
            row_copy(d, b).start()
        else:
            row_in[z] = row_out[b]

    collect("ctx", after_ref, link_s, link_r)
    tail = tail_decay(cum, doc)
    for h in range(heads):
        cols = cols_of(h)
        t = tail[:, h : h + 1]
        after = head_state(after_ref, h, heads)
        input_grad_ref[:, cols] = (input_ref[:, cols] + t * dot(write, after)).astype(BF16)
        write_part += dot_nt((x_ref[:, cols].astype(F32) * t).astype(BF16), after)

    share = length // crew
    maps[:, :, :DIM] = write_part.reshape(crew, share, DIM)
    maps[:, :, DIM:] = read_part.reshape(crew, share, DIM)
    maps_in[head] = maps[head]
    scatter("head", maps, maps_in, map_s, map_r)
    collect("head", maps_in, map_s, map_r)
    added = maps_in[0]
    for i in range(1, crew):
        added += maps_in[i]
    maps_sum[...] = added.astype(BF16)
    maps_all[head] = maps_sum[...]
    spread("head", maps_sum, maps_all, all_s, all_r)

    for d in range(1, ROW):
        z_from = ring(z, -d, ROW)
        send(row_out.at[z], row_in.at[z_from], row_s.at[d], row_r.at[d], ctx=x * ROW + z_from).wait_recv()
    for a in range(QUAD):
        both = row_in[a].astype(F32) + row_in[QUAD + a].astype(F32)
        key_grad_ref[:, cols_of(a)] = both[:, :DIM].astype(BF16)
        value_grad_ref[:, cols_of(a)] = both[:, DIM:].astype(BF16)

    collect("head", maps_all, all_s, all_r)
    both = maps_all[...].reshape(length, 2 * DIM)
    write_grad_ref[...] = both[:, :DIM]
    read_grad_ref[...] = both[:, DIM:]

    for d in range(QUAD):
        for copy in result_copies(d, ring(spot, -d, QUAD), spot):
            if d == 0:
                copy.wait()
            else:
                copy.wait_recv()

    for d in range(1, QUAD):
        for copy in result_copies(d, spot, ring(spot, d, QUAD)):
            copy.wait_send()
    for d in range(1, ROW):
        row_copy(d, ring(z, d, ROW)).wait_send()

    @pl.loop(0, ROW)
    def _(b):
        @pl.when((x >= 2) & wanted(b))
        def _():
            far(b).wait_send()

        @pl.when(x >= 1)
        def _():
            near(b).wait_send()

    settle("ctx", parts_out.at[0], part_s, part_r)
    settle("ctx", linked.at[0], link_s, link_r)
    settle("head", maps.at[0], map_s, map_r)
    settle("head", maps_sum, all_s, all_r)


def remote_call(kernel, number, outs, kept, args, far, scratch, sems):
    vmem, stay = pl.BlockSpec(memory_space=pltpu.VMEM), pl.BlockSpec(memory_space=pl.ANY)
    return pl.pallas_call(
        kernel,
        out_shape=tuple(outs),
        in_specs=[stay if i in far else vmem for i in range(len(args))],
        out_specs=tuple(stay if i in kept else vmem for i in range(len(outs))),
        scratch_shapes=[pltpu.VMEM(s, t) for s, t in scratch] + [pltpu.SemaphoreType.DMA(s) for s in sems],
        compiler_params=pltpu.CompilerParams(
            collective_id=number, has_side_effects=True, vmem_limit_bytes=VMEM_LIMIT
        ),
    )(*args)


def body(
    ssm_input,
    gate_input,
    write_map,
    read_map,
    log_decay,
    doc_start,
    ssm_grad,
    att_queries,
    att_keys,
    att_values,
    att_grad,
):
    ctx, crew = lax.axis_size("ctx"), lax.axis_size("head")
    length, width = ssm_input.shape
    heads = width // DIM
    att_width = att_queries.shape[1]
    part = (ctx, heads * DIM // ctx, DIM)
    flat, tall = (length, width), (length, DIM)

    kv, qg, facts, factor, cum, cum_t, doc_col, prior, mixed, sums = remote_call(
        forward_kernel,
        0,
        [
            shape((3 * SPAN, 2 * DIM), BF16), shape((QUAD * length, 2 * DIM), BF16),
            shape((ctx, 8, DIM), F32), shape((ctx, DIM), F32), shape((length, heads), F32),
            shape((heads, length), F32), shape((length, 1), F32), shape(part, BF16), shape(flat, F32),
            shape(tall, F32),
        ],
        (0, 1),
        (
            doc_start.reshape(2, length // 2), log_decay, ssm_input, gate_input, ssm_grad, write_map, read_map,
            att_queries, att_keys, att_values, att_grad,
        ),
        (7, 8, 9, 10),
        [((8, DIM), F32), (tall, F32), (part, BF16), (part, BF16), (part, BF16),
         ((8, length), F32), ((crew, 8, length), F32)],
        [(ROW, 2), (ROW, 2), (QUAD, 2), (QUAD, 2), (ROW,), (ROW,), (ROW,), (ROW,),
         (ctx,), (ctx,), (ctx,), (ctx,), (ctx,), (ctx,), (crew,), (crew,)],
    )

    og, dkv = attention(facts, qg, kv)

    block = (ROW, TOK, 2 * DIM)
    share = (crew, length // crew, 2 * DIM)
    return tuple(
        remote_call(
            functools.partial(backward_kernel, width * crew),
            1,
            [shape(flat, BF16), shape((length, att_width), BF16), shape(flat, BF16), shape(flat, BF16),
             shape(tall, BF16), shape(tall, BF16), shape((length, att_width), BF16),
             shape((length, att_width), BF16), shape((length, att_width), BF16)],
            (),
            (sums, mixed, ssm_input, gate_input, ssm_grad, write_map, read_map, cum, cum_t, doc_col, prior, factor,
             og, dkv),
            (),
            [(flat, BF16), (flat, F32), (part, BF16), (part, BF16), (part, BF16), (part, BF16),
             (share, F32), (share, F32), (share[1:], BF16), (share, BF16),
             (block, BF16), (block, BF16), (block, BF16), (block, BF16), (block, BF16)],
            [(QUAD, 2), (QUAD, 2), (ROW,), (ROW,), (ROW,), (ROW,), (ROW,), (ROW,),
             (ctx,), (ctx,), (ctx,), (ctx,), (crew,), (crew,), (crew,), (crew,)],
        )
    )


def solution(mesh):
    tokens, both = P("ctx", None), P("ctx", "head")
    in_specs = (both, both, tokens, tokens, both, P("ctx"), both, both, both, both, both)
    out_specs = (both, both, both, both, tokens, tokens, both, both, both)
    return jax.shard_map(body, mesh=mesh, in_specs=in_specs, out_specs=out_specs, check_vma=False)
```

```python
import functools
import math

import jax
import jax.numpy as jnp
from jax import lax
from jax.experimental import pallas as pl
from jax.experimental.pallas import tpu as pltpu
from jax.sharding import PartitionSpec as P

DIM = 128
WINDOW = 4096
EPSILON = 1e-05
ROW = 8
QUAD = 4
TQ = 256
TK = 512
QUERIES = QUAD * 256
HIDDEN = -1e30
F32 = jnp.float32
BF16 = jnp.bfloat16
EXACT = lax.Precision.HIGHEST
SCALE = DIM**-0.5
SCALE2 = SCALE * math.log2(math.e)
VMEM_LIMIT = 60 * 2**20
MESH = pl.DeviceIdType.MESH
TOK = 256
SPAN = ROW * TOK


def dot(a, b, precision=None):
    return jnp.dot(a, b, preferred_element_type=F32, precision=precision)


def dot_nt(a, b):
    return lax.dot_general(a, b, (((1,), (1,)), ((), ())), preferred_element_type=F32)


def dot_tn(a, b):
    return lax.dot_general(a, b, (((0,), (0,)), ((), ())), preferred_element_type=F32)


def shape(dims, dtype):
    return jax.ShapeDtypeStruct(dims, dtype)


def send(src, dst, sent, arrived, **where):
    return pltpu.make_async_remote_copy(
        src_ref=src, dst_ref=dst, send_sem=sent, recv_sem=arrived, device_id=where, device_id_type=MESH
    )


def ring(at, by, size):
    return lax.rem(at + by + size, size)


def greet():
    barrier = pltpu.get_barrier_semaphore()
    ctx, head = lax.axis_size("ctx"), lax.axis_size("head")
    for axis, size in (("ctx", ctx), ("head", head)):
        if size == 1:
            continue
        me = lax.axis_index(axis)

        @pl.loop(1, size)
        def _(d):
            pl.semaphore_signal(
                barrier, inc=1, device_id={axis: ring(me, d, size)}, device_id_type=MESH
            )

    pl.semaphore_wait(barrier, ctx + head - 2)


def scatter(axis, src, dst, sent, arrived):
    size, me = lax.axis_size(axis), lax.axis_index(axis)

    @pl.loop(1, size)
    def _(d):
        to = ring(me, d, size)
        send(src.at[to], dst.at[me], sent.at[d], arrived.at[d], **{axis: to}).start()


def spread(axis, src, dst, sent, arrived):
    size, me = lax.axis_size(axis), lax.axis_index(axis)

    @pl.loop(1, size)
    def _(d):
        send(src, dst.at[me], sent.at[d], arrived.at[d], **{axis: ring(me, d, size)}).start()


def collect(axis, dst, sent, arrived):
    size, me = lax.axis_size(axis), lax.axis_index(axis)

    @pl.loop(1, size)
    def _(d):
        block = dst.at[ring(me, -d, size)]
        send(block, block, sent.at[d], arrived.at[d], **{axis: ring(me, d, size)}).wait_recv()


def settle(axis, src, sent, arrived):
    size, me = lax.axis_size(axis), lax.axis_index(axis)

    @pl.loop(1, size)
    def _(d):
        send(src, src, sent.at[d], arrived.at[d], **{axis: ring(me, d, size)}).wait_send()


def column(row):
    n = row.shape[1]
    same = lax.broadcasted_iota(jnp.int32, (n, n), 0) == lax.broadcasted_iota(jnp.int32, (n, n), 1)
    return jnp.sum(jnp.where(same, row, 0.0), axis=1, keepdims=True)


def tail_decay(cum, doc):
    length = cum.shape[0]
    same = doc == doc[length - 1 : length, :]
    return jnp.where(same, jnp.exp(cum[length - 1 : length, :] - cum), 0.0)


def head_decay(cum, cum_t, seen, h):
    return jnp.exp(jnp.where(seen, cum[:, h : h + 1] - cum_t[h : h + 1, :], HIDDEN))


def visible(doc, start):
    length = doc.shape[0]
    row = lax.broadcasted_iota(jnp.int32, (length, length), 0)
    col = lax.broadcasted_iota(jnp.int32, (length, length), 1)
    return (row >= col) & ((start + col).astype(F32) >= doc)


def gate_terms(gate):
    sigma = jax.nn.sigmoid(gate)
    return sigma, gate * sigma


def cols_of(h):
    return slice(h * DIM, (h + 1) * DIM)


def head_state(buf, h, heads):
    share = buf.shape[0] // heads
    return buf[h * share : (h + 1) * share].reshape(DIM, DIM)


def put_state(buf, h, heads, value):
    share = buf.shape[0] // heads
    buf[h * share : (h + 1) * share] = value.astype(BF16).reshape(share, DIM // share, DIM)


def chain(parts, linked, factor, reverse):
    n = parts.shape[0]
    edge = n - 1 if reverse else 0
    linked[edge] = jnp.zeros(linked.shape[1:], BF16)

    def one(step, total):
        i = n - 1 - step if reverse else step
        total = total * factor[pl.ds(i, 1), :] + parts[i].astype(F32)
        linked[i - 1 if reverse else i + 1] = total.astype(BF16)
        return total

    lax.fori_loop(0, n - 1, one, jnp.zeros(parts.shape[1:], F32))


def rows_of(first, block):
    return pl.ds(pl.multiple_of(first + block * TOK, TOK), TOK)


def head_block(ref, a):
    return ref.at[:, pl.ds(pl.multiple_of(a * DIM, DIM), DIM)]


HALVES = (slice(0, DIM), slice(DIM, 2 * DIM))


def mixer_kernel(
    width, doc_ref, rate_ref, x_ref, gate_ref, grad_ref, write_ref, read_ref, q_ref, k_ref, v_ref, g_ref,
    out_ref, window_ref, input_grad_ref, gate_grad_ref, write_grad_ref, read_grad_ref,
    query_grad_ref, key_grad_ref, value_grad_ref,
    kv_ref, qg_ref, og_ref, facts_ref, factor_ref, fact, wide, mixed_ref, dmixed_ref, input_ref,
    parts_out, parts_in, linked, prior_ref, back_out, back_in, relinked, after_ref,
    sums_out, sums_in, maps, maps_in, maps_sum, maps_all,
    far_out, far_in, near_out, near_in, row_out, row_in,
    qt_ref, gt_ref, stat_ref, low_ref, out_t, dq_t, p_ref, ds_ref,
    kv_s, kv_r, qg_s, qg_r, one_s, one_r, two_s, two_r, og_s, og_r, far_s, far_r, near_s, near_r, row_s, row_r,
    fact_s, fact_r, part_s, part_r, link_s, link_r, back_s, back_r, relink_s, relink_r,
    sum_s, sum_r, map_s, map_r, all_s, all_r,
):
    ctx, crew = lax.axis_size("ctx"), lax.axis_size("head")
    me, head = lax.axis_index("ctx"), lax.axis_index("head")
    x, z = me // ROW, lax.rem(me, ROW)
    spot = lax.rem(me, QUAD)
    half = z // QUAD
    last_row = ctx // ROW - 1
    length, heads = rate_ref.shape
    start = me * length

    def key_copies(d, z_from, z_to):
        out = []
        for i, ref in enumerate((k_ref, v_ref)):
            src = head_block(ref, lax.rem(z_to, QUAD))
            dst = kv_ref.at[rows_of(2 * SPAN, z_from), HALVES[i]]
            if d == 0:
                out.append(pltpu.make_async_copy(src, dst, kv_r.at[d, i]))
            else:
                out.append(send(src, dst, kv_s.at[d, i], kv_r.at[d, i], ctx=x * ROW + z_to))
        return out

    def query_copies(d, from_, to):
        out = []
        for i, ref in enumerate((q_ref, g_ref)):
            src = head_block(ref, to)
            dst = qg_ref.at[rows_of(0, from_), HALVES[i]]
            if d == 0:
                out.append(pltpu.make_async_copy(src, dst, qg_r.at[d, i]))
            else:
                out.append(send(src, dst, qg_s.at[d, i], qg_r.at[d, i], ctx=me - spot + to))
        return out

    def pass_on(d, first, sent, arrived):
        z_from = ring(z, -d, ROW)
        return send(
            kv_ref.at[rows_of(first, z_from), :],
            kv_ref.at[rows_of(first - SPAN, z_from), :],
            sent.at[d], arrived.at[d], ctx=lax.rem(me + ROW, ctx),
        )

    def result_copy(i, d, a, to):
        src = og_ref.at[rows_of(0, to), HALVES[i]]
        dst = head_block((window_ref, query_grad_ref)[i], a)
        if d == 0:
            return pltpu.make_async_copy(src, dst, og_r.at[d, i])
        return send(src, dst, og_s.at[d, i], og_r.at[d, i], ctx=me - spot + to)

    def far(b):
        return send(far_out.at[b], far_in.at[b], far_s.at[b], far_r.at[b], ctx=lax.rem(me + ctx - ROW, ctx))

    def near(b):
        return send(near_out.at[b], near_in.at[b], near_s.at[b], near_r.at[b], ctx=lax.rem(me + ctx - ROW, ctx))

    def row_copy(d, b):
        return send(row_out.at[b], row_in.at[z], row_s.at[d], row_r.at[d], ctx=x * ROW + b)

    def wanted(b):
        return (z < QUAD) | (b >= QUAD)

    docs = doc_ref[...].astype(F32)
    rate = rate_ref[...]
    fact[...] = jnp.zeros_like(fact)
    fact[0:2, :] = docs
    fact[2:3, :heads] = jnp.sum(rate, axis=0, keepdims=True)
    facts_ref[me] = fact[...]

    greet()
    for d in range(ROW):
        for copy in key_copies(d, z, ring(z, d, ROW)):
            copy.start()
    spread("ctx", fact, facts_ref, fact_s, fact_r)

    row = lax.broadcasted_iota(jnp.int32, (length, length), 0)
    col = lax.broadcasted_iota(jnp.int32, (length, length), 1)
    cum = dot((row >= col).astype(F32), rate, EXACT)
    wide[...] = jnp.zeros_like(wide)
    wide[:, :heads] = cum
    cum_t = wide[...].T[:heads]
    doc = jnp.concatenate([column(docs[0:1, :]), column(docs[1:2, :])], axis=0)
    tail = tail_decay(cum, doc)
    enter = jnp.where(doc < start.astype(F32), jnp.exp(cum), 0.0)
    write, read = write_ref[...], read_ref[...]
    for h in range(heads):
        scaled = (x_ref[:, cols_of(h)].astype(F32) * tail[:, h : h + 1]).astype(BF16)
        put_state(parts_out, h, heads, dot_tn(write, scaled))
    parts_in[me] = parts_out[me]
    scatter("ctx", parts_out, parts_in, part_s, part_r)
    for d in range(QUAD):
        for copy in query_copies(d, spot, ring(spot, d, QUAD)):
            copy.start()

    def keys_arrived(d):
        for copy in key_copies(d, ring(z, -d, ROW), z):
            if d == 0:
                copy.wait()
            else:
                copy.wait_recv()

        @pl.when(x < last_row)
        def _():
            pass_on(d, 2 * SPAN, one_s, one_r).start()

    keys_arrived(0)

    seen = visible(doc, start)
    scores = dot_nt(read, write)
    for h in range(heads):
        mix = (head_decay(cum, cum_t, seen, h) * scores).astype(BF16)
        mixed_ref[:, cols_of(h)] = dot(mix, x_ref[:, cols_of(h)])

    collect("ctx", facts_ref, fact_s, fact_r)
    at = lax.broadcasted_iota(jnp.int32, (ctx, 1), 0)
    lane = lax.broadcasted_iota(jnp.int32, (ctx, DIM), 1)
    mine = me // (ctx // heads)
    total = jnp.sum(jnp.where(lane == mine, facts_ref[:, 2, :], 0.0), axis=1, keepdims=True)
    final = jnp.sum(jnp.where(lane == DIM - 1, facts_ref[:, 1, :], 0.0), axis=1, keepdims=True)
    factor = jnp.where(final < (at * length).astype(F32), jnp.exp(total), 0.0)
    factor_ref[...] = jnp.broadcast_to(factor, factor_ref.shape)

    for d in (1, 7, 2, 6):
        keys_arrived(d)
    collect("ctx", parts_in, part_s, part_r)
    chain(parts_in, linked, factor_ref, False)
    prior_ref[me] = linked[me]
    scatter("ctx", linked, prior_ref, link_s, link_r)
    for d in (3, 5, 4):
        keys_arrived(d)
    for d in range(QUAD):
        for copy in query_copies(d, ring(spot, -d, QUAD), spot):
            if d == 0:
                copy.wait()
            else:
                copy.wait_recv()

    first_key = half * QUERIES

    def keys_of(u):
        return pl.ds(pl.multiple_of(first_key + u * TK, TK), TK)

    def tile(j):
        return pl.ds(pl.multiple_of(j * TQ, TQ), TQ)

    for j in range(QUAD):
        cols = slice(j * TQ, (j + 1) * TQ)
        qt_ref[:, cols] = qg_ref[cols, :DIM].T
        gt_ref[:, cols] = qg_ref[cols, DIM:].T
        own = facts_ref[me - spot + j]
        own = jnp.concatenate([own[0:1, :], own[1:2, :]], axis=1).astype(jnp.int32)
        high = 2 * SPAN + first_key + j * TQ + lax.broadcasted_iota(jnp.int32, (1, TQ), 1)
        low_ref[0:1, cols] = jnp.maximum(own - (x - 2) * SPAN, high - (WINDOW - 1))
        low_ref[1:2, cols] = high
    stat_ref[0:1, :] = jnp.full((1, QUERIES), HIDDEN, F32)
    stat_ref[1:2, :] = jnp.zeros((1, QUERIES), F32)
    out_t[...] = jnp.zeros_like(out_t)
    dq_t[...] = jnp.zeros_like(dq_t)

    def score(u, j, edge):
        s = dot(kv_ref[keys_of(u), :DIM], qt_ref[:, tile(j)])
        at = first_key + u * TK + lax.broadcasted_iota(jnp.int32, (TK, TQ), 0)
        shown = at >= low_ref[0:1, tile(j)]
        if edge:
            shown = shown & (at <= low_ref[1:2, tile(j)])
        return jnp.where(shown, s, HIDDEN)

    def forward(u, j, values_t, edge):
        cols = tile(j)
        s = score(u, j, edge)
        top = stat_ref[0:1, cols]
        new = jnp.maximum(top, jnp.max(s, axis=0, keepdims=True))
        p = jnp.exp2((s - new) * SCALE2)
        keep = jnp.exp2((top - new) * SCALE2)
        stat_ref[0:1, cols] = new
        stat_ref[1:2, cols] = stat_ref[1:2, cols] * keep + jnp.sum(p, axis=0, keepdims=True)
        out_t[:, cols] = out_t[:, cols] * keep + dot(values_t, p.astype(BF16))

    def whole_forward(begin, end):
        @pl.loop(begin, end)
        def _(u):
            values_t = kv_ref[keys_of(u), DIM:].T
            for j in range(QUAD):
                forward(u, j, values_t, False)

    def tiles_of_edge(u):
        return (0, 2 * u + 2) if u < 2 else (2 * (u - 8), QUAD)

    def edge_forward(u):
        values_t = kv_ref[keys_of(u), DIM:].T

        @pl.loop(*tiles_of_edge(u))
        def _(j):
            forward(u, j, values_t, True)

    near_first, here_first = QUAD - 2 * half, 8 - 2 * half

    edge_forward(8)
    edge_forward(9)
    whole_forward(here_first, 8)

    collect("ctx", prior_ref, link_s, link_r)
    squares = jnp.zeros((length, 1), F32)
    inner = jnp.zeros((length, 1), F32)
    for h in range(heads):
        mixed = mixed_ref[:, cols_of(h)] + enter[:, h : h + 1] * dot(read, head_state(prior_ref, h, heads))
        mixed_ref[:, cols_of(h)] = mixed
        gated = mixed * gate_terms(gate_ref[:, cols_of(h)].astype(F32))[1]
        squares += jnp.sum(gated * gated, axis=1, keepdims=True)
        inner += jnp.sum(grad_ref[:, cols_of(h)].astype(F32) * gated, axis=1, keepdims=True)
    wide[:, 0:1] = squares
    wide[:, 1:2] = inner
    sums_out[...] = wide[...].T[:8]
    sums_in[head] = sums_out[...]
    spread("head", sums_out, sums_in, sum_s, sum_r)

    for d in (0, 1, 7, 2, 6, 3, 5, 4):

        @pl.when(x >= 1)
        def _():
            pass_on(d, 2 * SPAN, one_s, one_r).wait_recv()

        @pl.when((x >= 1) & (x < last_row) & wanted(ring(z, -d, ROW)))
        def _():
            pass_on(d, SPAN, two_s, two_r).start()

    @pl.when(x >= 1)
    def _():
        whole_forward(near_first, here_first)

    collect("head", sums_in, sum_s, sum_r)
    sums = sums_in[0]
    for i in range(1, crew):
        sums += sums_in[i]
    sums = jnp.concatenate([sums, jnp.zeros((DIM - 8, length), F32)], axis=0).T
    rms = lax.rsqrt(sums[:, 0:1] / width + EPSILON)
    pull = rms * rms * rms * sums[:, 1:2] / width
    for h in range(heads):
        cols = cols_of(h)
        mixed = mixed_ref[:, cols]
        gate = gate_ref[:, cols].astype(F32)
        sigma, swish = gate_terms(gate)
        gated = mixed * swish
        out_ref[:, cols] = (gated * rms).astype(BF16)
        dgated = rms * grad_ref[:, cols].astype(F32) - pull * gated
        dmixed = dgated * swish
        dmixed_ref[:, cols] = dmixed.astype(BF16)
        gate_grad_ref[:, cols] = (dgated * mixed * sigma * (1.0 + gate * (1.0 - sigma))).astype(BF16)
        put_state(back_out, h, heads, dot_tn(read, (enter[:, h : h + 1] * dmixed).astype(BF16)))
    back_in[me] = back_out[me]
    scatter("ctx", back_out, back_in, back_s, back_r)

    pairs = jnp.zeros_like(scores)
    read_part = jnp.zeros(read.shape, F32)
    for h in range(heads):
        cols = cols_of(h)
        decay = head_decay(cum, cum_t, seen, h)
        dmixed = dmixed_ref[:, cols]
        input_ref[:, cols] = dot_tn((decay * scores).astype(BF16), dmixed)
        pairs += decay * dot_nt(dmixed, x_ref[:, cols])
        entered = (enter[:, h : h + 1] * dmixed.astype(F32)).astype(BF16)
        read_part += dot_nt(entered, head_state(prior_ref, h, heads))
    pairs = pairs.astype(BF16)
    share = length // crew
    maps[:, :, :DIM] = dot_tn(pairs, read).reshape(crew, share, DIM)
    maps[:, :, DIM:] = (read_part + dot(pairs, write)).reshape(crew, share, DIM)

    collect("ctx", back_in, back_s, back_r)
    chain(back_in, relinked, factor_ref, True)
    after_ref[me] = relinked[me]
    scatter("ctx", relinked, after_ref, relink_s, relink_r)

    for d in (0, 1, 7, 2, 6, 3, 5, 4):

        @pl.when((x >= 2) & wanted(ring(z, -d, ROW)))
        def _():
            pass_on(d, SPAN, two_s, two_r).wait_recv()

    @pl.when(x >= 2)
    def _():
        whole_forward(2, near_first)
        edge_forward(0)
        edge_forward(1)

    for j in range(QUAD):
        cols = slice(j * TQ, (j + 1) * TQ)
        total = stat_ref[1:2, cols]
        attended = out_t[:, cols] / total
        og_ref[cols, :DIM] = attended.T.astype(BF16)
        stat_ref[2:3, cols] = stat_ref[0:1, cols] * SCALE2 + jnp.log2(total)
        stat_ref[3:4, cols] = jnp.sum(gt_ref[:, cols].astype(F32) * attended, axis=0, keepdims=True)
    for d in range(QUAD):
        result_copy(0, d, spot, ring(spot, d, QUAD)).start()

    def backward(u, j, edge):
        cols = tile(j)
        p = jnp.exp2(score(u, j, edge) * SCALE2 - stat_ref[2:3, cols])
        dp = dot(kv_ref[keys_of(u), DIM:], gt_ref[:, cols])
        p_ref[:, cols] = p.astype(BF16)
        ds_ref[:, cols] = (p * (dp - stat_ref[3:4, cols])).astype(BF16)

    def gather_backward(u):
        dq_t[...] += dot(kv_ref[keys_of(u), :DIM].T, ds_ref[...])
        return dot(ds_ref[...], qg_ref[:, :DIM]) * SCALE, dot(p_ref[...], qg_ref[:, DIM:])

    def whole_backward(begin, end, emit):
        @pl.loop(begin, end)
        def _(u):
            for j in range(QUAD):
                backward(u, j, False)
            emit(u, *gather_backward(u))

    def edge_backward(u, emit):
        begin, end = tiles_of_edge(u)
        if end - begin < QUAD:
            p_ref[...] = jnp.zeros_like(p_ref)
            ds_ref[...] = jnp.zeros_like(ds_ref)

        @pl.loop(begin, end)
        def _(j):
            backward(u, j, True)

        emit(u, *gather_backward(u))

    def blocks_of(u, dk, dv):
        b = lax.rem(2 * u + QUAD * half, ROW)
        both = jnp.concatenate([dk, dv], axis=1)
        return (b, both[:TOK]), (b + 1, both[TOK:])

    def emit_far(u, dk, dv):
        for b, part in blocks_of(u, dk, dv):
            far_out[b] = part.astype(BF16)
            far(b).start()

    def pass_near(b, part):
        more = (x < last_row) & wanted(b)
        near_out[b] = part.astype(BF16)

        @pl.when(more)
        def _():
            far(b).wait_recv()
            near_out[b] = (part + far_in[b].astype(F32)).astype(BF16)

        near(b).start()

    def emit_near(u, dk, dv):
        for b, part in blocks_of(u, dk, dv):
            pass_near(b, part)

    def pass_row(b, part):
        row_out[b] = part.astype(BF16)

        @pl.when(x < last_row)
        def _():
            near(b).wait_recv()
            row_out[b] = (part + near_in[b].astype(F32)).astype(BF16)

        @pl.when(b != z)
        def _():
            row_copy(ring(b, -z, ROW), b).start()

        @pl.when(b == z)
        def _():
            row_in[z] = row_out[b]

    def emit_row(u, dk, dv):
        for b, part in blocks_of(u, dk, dv):
            pass_row(b, part)

    @pl.when(x >= 2)
    def _():
        edge_backward(0, emit_far)
        edge_backward(1, emit_far)
        whole_backward(2, near_first, emit_far)

    @pl.when(x >= 1)
    def _():
        whole_backward(near_first, here_first, emit_near)

    collect("ctx", after_ref, relink_s, relink_r)
    write_part = maps[:, :, :DIM].reshape(length, DIM)
    for h in range(heads):
        cols = cols_of(h)
        t = tail[:, h : h + 1]
        after = head_state(after_ref, h, heads)
        input_grad_ref[:, cols] = (input_ref[:, cols] + t * dot(write, after)).astype(BF16)
        write_part += dot_nt((x_ref[:, cols].astype(F32) * t).astype(BF16), after)

    maps[:, :, :DIM] = write_part.reshape(crew, share, DIM)
    maps_in[head] = maps[head]
    scatter("head", maps, maps_in, map_s, map_r)

    whole_backward(here_first, 8, emit_row)
    edge_backward(8, emit_row)
    edge_backward(9, emit_row)

    for j in range(QUAD):
        cols = slice(j * TQ, (j + 1) * TQ)
        og_ref[cols, DIM:] = (dq_t[:, cols] * SCALE).T.astype(BF16)
    for d in range(QUAD):
        result_copy(1, d, spot, ring(spot, d, QUAD)).start()

    @pl.when(half == 0)
    def _():
        @pl.loop(QUAD, ROW)
        def _(b):
            pass_row(b, jnp.zeros((TOK, 2 * DIM), F32))

    collect("head", maps_in, map_s, map_r)
    added = maps_in[0]
    for i in range(1, crew):
        added += maps_in[i]
    maps_sum[...] = added.astype(BF16)
    maps_all[head] = maps_sum[...]
    spread("head", maps_sum, maps_all, all_s, all_r)

    for d in range(1, ROW):
        z_from = ring(z, -d, ROW)
        send(row_out.at[z], row_in.at[z_from], row_s.at[d], row_r.at[d], ctx=x * ROW + z_from).wait_recv()
    for a in range(QUAD):
        both = row_in[a].astype(F32) + row_in[QUAD + a].astype(F32)
        key_grad_ref[:, cols_of(a)] = both[:, :DIM].astype(BF16)
        value_grad_ref[:, cols_of(a)] = both[:, DIM:].astype(BF16)

    collect("head", maps_all, all_s, all_r)
    both = maps_all[...].reshape(length, 2 * DIM)
    write_grad_ref[...] = both[:, :DIM]
    read_grad_ref[...] = both[:, DIM:]

    for i in range(2):
        for d in range(QUAD):
            copy = result_copy(i, d, ring(spot, -d, QUAD), spot)
            if d == 0:
                copy.wait()
            else:
                copy.wait_recv()

    for d in range(1, ROW):
        for copy in key_copies(d, z, ring(z, d, ROW)):
            copy.wait_send()
        row_copy(d, ring(z, d, ROW)).wait_send()
    for d in range(1, QUAD):
        for copy in query_copies(d, spot, ring(spot, d, QUAD)):
            copy.wait_send()
        for i in range(2):
            result_copy(i, d, spot, ring(spot, d, QUAD)).wait_send()

    @pl.loop(0, ROW)
    def _(d):
        @pl.when(x < last_row)
        def _():
            pass_on(d, 2 * SPAN, one_s, one_r).wait_send()

        @pl.when((x >= 1) & (x < last_row) & wanted(ring(z, -d, ROW)))
        def _():
            pass_on(d, SPAN, two_s, two_r).wait_send()

        @pl.when((x >= 2) & wanted(d))
        def _():
            far(d).wait_send()

        @pl.when(x >= 1)
        def _():
            near(d).wait_send()

    settle("ctx", fact, fact_s, fact_r)
    settle("ctx", parts_out.at[0], part_s, part_r)
    settle("ctx", linked.at[0], link_s, link_r)
    settle("ctx", back_out.at[0], back_s, back_r)
    settle("ctx", relinked.at[0], relink_s, relink_r)
    settle("head", sums_out, sum_s, sum_r)
    settle("head", maps.at[0], map_s, map_r)
    settle("head", maps_sum, all_s, all_r)


def deliver_kernel(*refs):
    n = len(refs) // 2
    for src, dst in zip(refs[:n], refs[n:]):
        dst[...] = src[...]


def body(
    ssm_input,
    gate_input,
    write_map,
    read_map,
    log_decay,
    doc_start,
    ssm_grad,
    att_queries,
    att_keys,
    att_values,
    att_grad,
):
    ctx, crew = lax.axis_size("ctx"), lax.axis_size("head")
    length, width = ssm_input.shape
    heads = width // DIM
    flat, tall, attended = (length, width), (length, DIM), att_queries.shape
    part = (ctx, heads * DIM // ctx, DIM)
    block = (ROW, TOK, 2 * DIM)
    share = (crew, length // crew, 2 * DIM)
    outs = [shape(s, BF16) for s in (flat, attended, flat, flat, tall, tall, attended, attended, attended)]
    vmem, stay = pl.BlockSpec(memory_space=pltpu.VMEM), pl.BlockSpec(memory_space=pl.ANY)
    scratch = [
        ((3 * SPAN, 2 * DIM), BF16), ((QUERIES, 2 * DIM), BF16), ((QUERIES, 2 * DIM), BF16),
        ((ctx, 8, DIM), F32), ((ctx, DIM), F32), ((8, DIM), F32), (tall, F32), (flat, F32), (flat, BF16), (flat, F32),
        *[(part, BF16)] * 8,
        ((8, length), F32), ((crew, 8, length), F32), (share, F32), (share, F32), (share[1:], BF16), (share, BF16),
        *[(block, BF16)] * 6,
        ((DIM, QUERIES), BF16), ((DIM, QUERIES), BF16), ((8, QUERIES), F32), ((8, QUERIES), jnp.int32),
        ((DIM, QUERIES), F32), ((DIM, QUERIES), F32), ((TK, QUERIES), BF16), ((TK, QUERIES), BF16),
    ]
    sems = [(ROW, 2)] * 2 + [(QUAD, 2)] * 2 + [(ROW,)] * 4 + [(QUAD, 2)] * 2 + [(ROW,)] * 6
    sems += [(ctx,)] * 10 + [(crew,)] * 6
    found = pl.pallas_call(
        functools.partial(mixer_kernel, width * crew),
        out_shape=tuple(outs),
        in_specs=[vmem] * 7 + [stay] * 4,
        out_specs=(vmem,) * len(outs),
        scratch_shapes=[pltpu.VMEM(s, t) for s, t in scratch] + [pltpu.SemaphoreType.DMA(s) for s in sems],
        compiler_params=pltpu.CompilerParams(
            collective_id=0, has_side_effects=True, vmem_limit_bytes=VMEM_LIMIT
        ),
    )(
        doc_start.reshape(2, length // 2), log_decay, ssm_input, gate_input, ssm_grad, write_map, read_map,
        att_queries, att_keys, att_values, att_grad,
    )
    return pl.pallas_call(
        deliver_kernel,
        out_shape=tuple(outs),
        in_specs=[vmem] * len(outs),
        out_specs=(vmem,) * len(outs),
    )(*found)


def solution(mesh):
    tokens, both = P("ctx", None), P("ctx", "head")
    in_specs = (both, both, tokens, tokens, both, P("ctx"), both, both, both, both, both)
    out_specs = (both, both, both, both, tokens, tokens, both, both, both)
    return jax.shard_map(body, mesh=mesh, in_specs=in_specs, out_specs=out_specs, check_vma=False)
```

```python
import functools
import math

import jax
import jax.numpy as jnp
from jax import lax
from jax.experimental import pallas as pl
from jax.experimental.pallas import tpu as pltpu
from jax.sharding import PartitionSpec as P

DIM = 128
WINDOW = 4096
EPSILON = 1e-05
ROW = 8
QUAD = 4
TQ = 256
TK = 512
QUERIES = QUAD * 256
HIDDEN = -1e30
F32 = jnp.float32
BF16 = jnp.bfloat16
EXACT = lax.Precision.HIGHEST
SCALE = DIM**-0.5
SCALE2 = SCALE * math.log2(math.e)
VMEM_LIMIT = 60 * 2**20
MESH = pl.DeviceIdType.MESH
TOK = 256
SPAN = ROW * TOK


def dot(a, b, precision=None):
    return jnp.dot(a, b, preferred_element_type=F32, precision=precision)


def dot_nt(a, b):
    return lax.dot_general(a, b, (((1,), (1,)), ((), ())), preferred_element_type=F32)


def dot_tn(a, b):
    return lax.dot_general(a, b, (((0,), (0,)), ((), ())), preferred_element_type=F32)


def shape(dims, dtype):
    return jax.ShapeDtypeStruct(dims, dtype)


def send(src, dst, sent, arrived, **where):
    return pltpu.make_async_remote_copy(
        src_ref=src, dst_ref=dst, send_sem=sent, recv_sem=arrived, device_id=where, device_id_type=MESH
    )


def ring(at, by, size):
    return lax.rem(at + by + size, size)


def greet():
    barrier = pltpu.get_barrier_semaphore()
    ctx, head = lax.axis_size("ctx"), lax.axis_size("head")
    for axis, size in (("ctx", ctx), ("head", head)):
        if size == 1:
            continue
        me = lax.axis_index(axis)

        @pl.loop(1, size)
        def _(d):
            pl.semaphore_signal(
                barrier, inc=1, device_id={axis: ring(me, d, size)}, device_id_type=MESH
            )


def await_greetings():
    pl.semaphore_wait(pltpu.get_barrier_semaphore(), lax.axis_size("ctx") + lax.axis_size("head") - 2)


def scatter(axis, src, dst, sent, arrived):
    size, me = lax.axis_size(axis), lax.axis_index(axis)

    @pl.loop(1, size)
    def _(d):
        to = ring(me, d, size)
        send(src.at[to], dst.at[me], sent.at[d], arrived.at[d], **{axis: to}).start()


def spread(axis, src, dst, sent, arrived):
    size, me = lax.axis_size(axis), lax.axis_index(axis)

    @pl.loop(1, size)
    def _(d):
        send(src, dst.at[me], sent.at[d], arrived.at[d], **{axis: ring(me, d, size)}).start()


def collect(axis, dst, sent, arrived):
    size, me = lax.axis_size(axis), lax.axis_index(axis)

    @pl.loop(1, size)
    def _(d):
        block = dst.at[ring(me, -d, size)]
        send(block, block, sent.at[d], arrived.at[d], **{axis: ring(me, d, size)}).wait_recv()


def settle(axis, src, sent, arrived):
    size, me = lax.axis_size(axis), lax.axis_index(axis)

    @pl.loop(1, size)
    def _(d):
        send(src, src, sent.at[d], arrived.at[d], **{axis: ring(me, d, size)}).wait_send()


def column(row):
    n = row.shape[1]
    same = lax.broadcasted_iota(jnp.int32, (n, n), 0) == lax.broadcasted_iota(jnp.int32, (n, n), 1)
    return jnp.sum(jnp.where(same, row, 0.0), axis=1, keepdims=True)


def tail_decay(cum, doc):
    length = cum.shape[0]
    same = doc == doc[length - 1 : length, :]
    return jnp.where(same, jnp.exp(cum[length - 1 : length, :] - cum), 0.0)


def head_decay(cum, cum_t, seen, h):
    return jnp.exp(jnp.where(seen, cum[:, h : h + 1] - cum_t[h : h + 1, :], HIDDEN))


def visible(doc, start):
    length = doc.shape[0]
    row = lax.broadcasted_iota(jnp.int32, (length, length), 0)
    col = lax.broadcasted_iota(jnp.int32, (length, length), 1)
    return (row >= col) & ((start + col).astype(F32) >= doc)


def gate_terms(gate):
    sigma = jax.nn.sigmoid(gate)
    return sigma, gate * sigma


def cols_of(h):
    return slice(h * DIM, (h + 1) * DIM)


def head_state(buf, h, heads):
    share = buf.shape[0] // heads
    return buf[h * share : (h + 1) * share].reshape(DIM, DIM)


def put_state(buf, h, heads, value):
    share = buf.shape[0] // heads
    buf[h * share : (h + 1) * share] = value.astype(BF16).reshape(share, DIM // share, DIM)


def chain(parts, linked, factor, reverse):
    n = parts.shape[0]
    edge = n - 1 if reverse else 0
    linked[edge] = jnp.zeros(linked.shape[1:], BF16)

    def one(step, total):
        i = n - 1 - step if reverse else step
        total = total * factor[pl.ds(i, 1), :] + parts[i].astype(F32)
        linked[i - 1 if reverse else i + 1] = total.astype(BF16)
        return total

    lax.fori_loop(0, n - 1, one, jnp.zeros(parts.shape[1:], F32))


def rows_of(first, block):
    return pl.ds(pl.multiple_of(first + block * TOK, TOK), TOK)


def head_block(ref, a):
    return ref.at[:, pl.ds(pl.multiple_of(a * DIM, DIM), DIM)]


HALVES = (slice(0, DIM), slice(DIM, 2 * DIM))
NEAREST = (0, 1, 7, 2, 6, 3, 5, 4)


def mixer_kernel(
    width, doc_ref, rate_ref, x_ref, gate_ref, grad_ref, write_ref, read_ref, q_ref, k_ref, v_ref, g_ref,
    out_ref, window_ref, input_grad_ref, gate_grad_ref, write_grad_ref, read_grad_ref,
    query_grad_ref, key_grad_ref, value_grad_ref,
    kv_ref, relay_ref, qg_ref, og_ref, facts_ref, factor_ref, fact, wide, turned, mixed_ref, dmixed_ref, input_ref,
    parts_out, parts_in, linked, prior_ref, back_out, back_in, relinked, after_ref,
    sums_out, sums_in, maps, maps_in, maps_sum, maps_all,
    far_out, far_in, bend_ref, near_out, near_in, row_out, row_in,
    qt_ref, gt_ref, stat_ref, low_ref, out_t, dq_t, p_ref, ds_ref,
    kv_s, kv_r, qg_s, qg_r, one_s, one_r, two_s, two_r, turn_s, turn_r, og_s, og_r,
    far_s, far_r, bend_s, bend_r, near_s, near_r, row_s, row_r,
    fact_s, fact_r, part_s, part_r, link_s, link_r, back_s, back_r, relink_s, relink_r,
    sum_s, sum_r, map_s, map_r, all_s, all_r,
):
    ctx, crew = lax.axis_size("ctx"), lax.axis_size("head")
    me, head = lax.axis_index("ctx"), lax.axis_index("head")
    x, z = me // ROW, lax.rem(me, ROW)
    spot = lax.rem(me, QUAD)
    half = z // QUAD
    last_row = ctx // ROW - 1
    heads, length = rate_ref.shape
    start = me * length

    def key_copies(d, z_from, z_to):
        out = []
        for i, ref in enumerate((k_ref, v_ref)):
            src = head_block(ref, lax.rem(z_to, QUAD))
            dst = kv_ref.at[rows_of(2 * SPAN, z_from), HALVES[i]]
            if d == 0:
                out.append(pltpu.make_async_copy(src, dst, kv_r.at[d, i]))
            else:
                out.append(send(src, dst, kv_s.at[d, i], kv_r.at[d, i], ctx=x * ROW + z_to))
        return out

    def query_copies(d, from_, to):
        out = []
        for i, ref in enumerate((q_ref, g_ref)):
            src = head_block(ref, to)
            dst = qg_ref.at[rows_of(0, from_), HALVES[i]]
            if d == 0:
                out.append(pltpu.make_async_copy(src, dst, qg_r.at[d, i]))
            else:
                out.append(send(src, dst, qg_s.at[d, i], qg_r.at[d, i], ctx=me - spot + to))
        return out

    def row_at(by):
        return lax.rem(me + by * ROW + ctx, ctx)

    def one_on(b):
        return send(
            kv_ref.at[rows_of(2 * SPAN, b), :], kv_ref.at[rows_of(SPAN, b), :],
            one_s.at[b], one_r.at[b], ctx=row_at(1),
        )

    def two_on(b):
        return send(
            kv_ref.at[rows_of(2 * SPAN, b), :], kv_ref.at[rows_of(0, b), :],
            two_s.at[b], two_r.at[b], ctx=row_at(2),
        )

    def turn_in(b):
        return send(
            kv_ref.at[rows_of(2 * SPAN, b), :], relay_ref.at[lax.rem(b, QUAD)],
            turn_s.at[b], turn_r.at[b], ctx=row_at(-1),
        )

    def turn_out(b):
        return send(
            relay_ref.at[lax.rem(b, QUAD)], kv_ref.at[rows_of(0, b), :],
            two_s.at[b], two_r.at[b], ctx=row_at(-1),
        )

    def relayed(b):
        return (z < QUAD) & (b >= QUAD)

    relays = (x == last_row) | (x + 1 < last_row - 1)

    def result_copy(i, d, a, to):
        src = og_ref.at[rows_of(0, to), HALVES[i]]
        dst = head_block((window_ref, query_grad_ref)[i], a)
        if d == 0:
            return pltpu.make_async_copy(src, dst, og_r.at[d, i])
        return send(src, dst, og_s.at[d, i], og_r.at[d, i], ctx=me - spot + to)

    def far(b):
        return send(far_out.at[b], far_in.at[b], far_s.at[b], far_r.at[b], ctx=row_at(-2))

    def bend_in(b):
        return send(far_out.at[b], bend_ref.at[lax.rem(b, QUAD)], bend_s.at[b], bend_r.at[b], ctx=row_at(1))

    def bend_out(b):
        return send(bend_ref.at[lax.rem(b, QUAD)], far_in.at[b], far_s.at[b], far_r.at[b], ctx=row_at(1))

    def near(b):
        return send(near_out.at[b], near_in.at[b], near_s.at[b], near_r.at[b], ctx=row_at(-1))

    def row_copy(d, b):
        return send(row_out.at[b], row_in.at[z], row_s.at[d], row_r.at[d], ctx=x * ROW + b)

    def wanted(b):
        return (z < QUAD) | (b >= QUAD)

    greet()

    docs = doc_ref[...].astype(F32)
    row = lax.broadcasted_iota(jnp.int32, (length, length), 0)
    col = lax.broadcasted_iota(jnp.int32, (length, length), 1)
    cum_t = dot(rate_ref[...], (row <= col).astype(F32), EXACT)
    turned[...] = jnp.zeros_like(turned)
    turned[:heads, :] = cum_t
    cum = turned[...].T[:, :heads]
    fact[...] = jnp.zeros_like(fact)
    fact[0:2, :] = docs
    fact[2:3, :heads] = cum[length - 1 : length, :]
    facts_ref[me] = fact[...]

    doc = jnp.concatenate([column(docs[0:1, :]), column(docs[1:2, :])], axis=0)
    tail = tail_decay(cum, doc)
    enter = jnp.where(doc < start.astype(F32), jnp.exp(cum), 0.0)
    write, read = write_ref[...], read_ref[...]
    for h in range(heads):
        scaled = (x_ref[:, cols_of(h)].astype(F32) * tail[:, h : h + 1]).astype(BF16)
        put_state(parts_out, h, heads, dot_tn(write, scaled))
    parts_in[me] = parts_out[me]
    await_greetings()
    scatter("ctx", parts_out, parts_in, part_s, part_r)
    spread("ctx", fact, facts_ref, fact_s, fact_r)
    for d in NEAREST[:5]:
        for copy in key_copies(d, z, ring(z, d, ROW)):
            copy.start()

    seen = visible(doc, start)
    scores = dot_nt(read, write)
    for h in range(heads):
        mix = (head_decay(cum, cum_t, seen, h) * scores).astype(BF16)
        mixed_ref[:, cols_of(h)] = dot(mix, x_ref[:, cols_of(h)])

    collect("ctx", facts_ref, fact_s, fact_r)
    at = lax.broadcasted_iota(jnp.int32, (ctx, 1), 0)
    lane = lax.broadcasted_iota(jnp.int32, (ctx, DIM), 1)
    mine = me // (ctx // heads)
    total = jnp.sum(jnp.where(lane == mine, facts_ref[:, 2, :], 0.0), axis=1, keepdims=True)
    final = jnp.sum(jnp.where(lane == DIM - 1, facts_ref[:, 1, :], 0.0), axis=1, keepdims=True)
    factor = jnp.where(final < (at * length).astype(F32), jnp.exp(total), 0.0)
    factor_ref[...] = jnp.broadcast_to(factor, factor_ref.shape)

    collect("ctx", parts_in, part_s, part_r)
    chain(parts_in, linked, factor_ref, False)
    prior_ref[me] = linked[me]
    scatter("ctx", linked, prior_ref, link_s, link_r)
    for d in NEAREST[5:]:
        for copy in key_copies(d, z, ring(z, d, ROW)):
            copy.start()
    for d in range(QUAD):
        for copy in query_copies(d, spot, ring(spot, d, QUAD)):
            copy.start()

    def keys_arrived(d):
        b = ring(z, -d, ROW)
        for copy in key_copies(d, b, z):
            if d == 0:
                copy.wait()
            else:
                copy.wait_recv()

        @pl.when((x < last_row - 1) & relayed(b))
        def _():
            turn_in(b).start()

        @pl.when(x < last_row)
        def _():
            one_on(b).start()

        @pl.when((x < last_row - 1) & wanted(b) & jnp.logical_not(relayed(b)))
        def _():
            two_on(b).start()

    for d in NEAREST[:5]:
        keys_arrived(d)

    collect("ctx", prior_ref, link_s, link_r)
    squares = jnp.zeros((length, 1), F32)
    inner = jnp.zeros((length, 1), F32)
    for h in range(heads):
        mixed = mixed_ref[:, cols_of(h)] + enter[:, h : h + 1] * dot(read, head_state(prior_ref, h, heads))
        mixed_ref[:, cols_of(h)] = mixed
        gated = mixed * gate_terms(gate_ref[:, cols_of(h)].astype(F32))[1]
        squares += jnp.sum(gated * gated, axis=1, keepdims=True)
        inner += jnp.sum(grad_ref[:, cols_of(h)].astype(F32) * gated, axis=1, keepdims=True)
    wide[...] = jnp.zeros_like(wide)
    wide[:, 0:1] = squares
    wide[:, 1:2] = inner
    sums_out[...] = wide[...].T[:8]
    sums_in[head] = sums_out[...]
    spread("head", sums_out, sums_in, sum_s, sum_r)

    for d in NEAREST[5:]:
        keys_arrived(d)

    collect("head", sums_in, sum_s, sum_r)
    sums = sums_in[0]
    for i in range(1, crew):
        sums += sums_in[i]
    sums = jnp.concatenate([sums, jnp.zeros((DIM - 8, length), F32)], axis=0).T
    rms = lax.rsqrt(sums[:, 0:1] / width + EPSILON)
    pull = rms * rms * rms * sums[:, 1:2] / width
    for h in range(heads):
        cols = cols_of(h)
        mixed = mixed_ref[:, cols]
        gate = gate_ref[:, cols].astype(F32)
        sigma, swish = gate_terms(gate)
        gated = mixed * swish
        out_ref[:, cols] = (gated * rms).astype(BF16)
        dgated = rms * grad_ref[:, cols].astype(F32) - pull * gated
        dmixed = dgated * swish
        dmixed_ref[:, cols] = dmixed.astype(BF16)
        gate_grad_ref[:, cols] = (dgated * mixed * sigma * (1.0 + gate * (1.0 - sigma))).astype(BF16)
        put_state(back_out, h, heads, dot_tn(read, (enter[:, h : h + 1] * dmixed).astype(BF16)))
    back_in[me] = back_out[me]
    scatter("ctx", back_out, back_in, back_s, back_r)

    @pl.loop(QUAD, ROW)
    def _(b):
        @pl.when(relays & relayed(b))
        def _():
            turn_in(b).wait_recv()
            turn_out(b).start()

    pairs = jnp.zeros_like(scores)
    read_part = jnp.zeros(read.shape, F32)
    for h in range(heads):
        cols = cols_of(h)
        decay = head_decay(cum, cum_t, seen, h)
        dmixed = dmixed_ref[:, cols]
        input_ref[:, cols] = dot_tn((decay * scores).astype(BF16), dmixed)
        pairs += decay * dot_nt(dmixed, x_ref[:, cols])
        entered = (enter[:, h : h + 1] * dmixed.astype(F32)).astype(BF16)
        read_part += dot_nt(entered, head_state(prior_ref, h, heads))
    pairs = pairs.astype(BF16)
    share = length // crew
    maps[:, :, :DIM] = dot_tn(pairs, read).reshape(crew, share, DIM)
    maps[:, :, DIM:] = (read_part + dot(pairs, write)).reshape(crew, share, DIM)

    collect("ctx", back_in, back_s, back_r)
    chain(back_in, relinked, factor_ref, True)
    after_ref[me] = relinked[me]
    scatter("ctx", relinked, after_ref, relink_s, relink_r)

    for d in range(QUAD):
        for copy in query_copies(d, ring(spot, -d, QUAD), spot):
            if d == 0:
                copy.wait()
            else:
                copy.wait_recv()

    first_key = half * QUERIES

    def keys_of(u):
        return pl.ds(pl.multiple_of(first_key + u * TK, TK), TK)

    def tile(j):
        return pl.ds(pl.multiple_of(j * TQ, TQ), TQ)

    for j in range(QUAD):
        cols = slice(j * TQ, (j + 1) * TQ)
        qt_ref[:, cols] = qg_ref[cols, :DIM].T
        gt_ref[:, cols] = qg_ref[cols, DIM:].T
        own = facts_ref[me - spot + j]
        own = jnp.concatenate([own[0:1, :], own[1:2, :]], axis=1).astype(jnp.int32)
        high = 2 * SPAN + first_key + j * TQ + lax.broadcasted_iota(jnp.int32, (1, TQ), 1)
        low_ref[0:1, cols] = jnp.maximum(own - (x - 2) * SPAN, high - (WINDOW - 1))
        low_ref[1:2, cols] = high
    stat_ref[0:1, :] = jnp.full((1, QUERIES), HIDDEN, F32)
    stat_ref[1:2, :] = jnp.zeros((1, QUERIES), F32)
    out_t[...] = jnp.zeros_like(out_t)
    dq_t[...] = jnp.zeros_like(dq_t)

    def score(u, j, edge):
        s = dot(kv_ref[keys_of(u), :DIM], qt_ref[:, tile(j)])
        at = first_key + u * TK + lax.broadcasted_iota(jnp.int32, (TK, TQ), 0)
        shown = at >= low_ref[0:1, tile(j)]
        if edge:
            shown = shown & (at <= low_ref[1:2, tile(j)])
        return jnp.where(shown, s, HIDDEN)

    def forward(u, j, values_t, edge):
        cols = tile(j)
        s = score(u, j, edge)
        top = stat_ref[0:1, cols]
        new = jnp.maximum(top, jnp.max(s, axis=0, keepdims=True))
        p = jnp.exp2((s - new) * SCALE2)
        keep = jnp.exp2((top - new) * SCALE2)
        stat_ref[0:1, cols] = new
        stat_ref[1:2, cols] = stat_ref[1:2, cols] * keep + jnp.sum(p, axis=0, keepdims=True)
        out_t[:, cols] = out_t[:, cols] * keep + dot(values_t, p.astype(BF16))

    def whole_forward(begin, end):
        @pl.loop(begin, end)
        def _(u):
            values_t = kv_ref[keys_of(u), DIM:].T
            for j in range(QUAD):
                forward(u, j, values_t, False)

    def tiles_of_edge(u):
        return (0, 2 * u + 2) if u < 2 else (2 * (u - 8), QUAD)

    def edge_forward(u):
        values_t = kv_ref[keys_of(u), DIM:].T

        @pl.loop(*tiles_of_edge(u))
        def _(j):
            forward(u, j, values_t, True)

    near_first, here_first = QUAD - 2 * half, 8 - 2 * half

    edge_forward(8)
    edge_forward(9)

    whole_forward(here_first, 8)

    @pl.when(x >= 1)
    def _():
        @pl.loop(0, ROW)
        def _(b):
            one_on(b).wait_recv()

        whole_forward(near_first, here_first)

    @pl.when(x >= 2)
    def _():
        @pl.loop(0, ROW)
        def _(b):
            @pl.when(wanted(b))
            def _():
                two_on(b).wait_recv()

        whole_forward(2, near_first)
        edge_forward(0)
        edge_forward(1)

    for j in range(QUAD):
        cols = slice(j * TQ, (j + 1) * TQ)
        total = stat_ref[1:2, cols]
        attended = out_t[:, cols] / total
        og_ref[cols, :DIM] = attended.T.astype(BF16)
        stat_ref[2:3, cols] = stat_ref[0:1, cols] * SCALE2 + jnp.log2(total)
        stat_ref[3:4, cols] = jnp.sum(gt_ref[:, cols].astype(F32) * attended, axis=0, keepdims=True)
    for d in range(QUAD):
        result_copy(0, d, spot, ring(spot, d, QUAD)).start()

    def backward(u, j, edge):
        cols = tile(j)
        p = jnp.exp2(score(u, j, edge) * SCALE2 - stat_ref[2:3, cols])
        dp = dot(kv_ref[keys_of(u), DIM:], gt_ref[:, cols])
        p_ref[:, cols] = p.astype(BF16)
        ds_ref[:, cols] = (p * (dp - stat_ref[3:4, cols])).astype(BF16)

    def gather_backward(u):
        dq_t[...] += dot(kv_ref[keys_of(u), :DIM].T, ds_ref[...])
        return dot(ds_ref[...], qg_ref[:, :DIM]) * SCALE, dot(p_ref[...], qg_ref[:, DIM:])

    def whole_backward(begin, end, emit):
        @pl.loop(begin, end)
        def _(u):
            for j in range(QUAD):
                backward(u, j, False)
            emit(u, *gather_backward(u))

    def edge_backward(u, emit):
        begin, end = tiles_of_edge(u)
        if end - begin < QUAD:
            p_ref[...] = jnp.zeros_like(p_ref)
            ds_ref[...] = jnp.zeros_like(ds_ref)

        @pl.loop(begin, end)
        def _(j):
            backward(u, j, True)

        emit(u, *gather_backward(u))

    def blocks_of(u, dk, dv):
        b = lax.rem(2 * u + QUAD * half, ROW)
        both = jnp.concatenate([dk, dv], axis=1)
        return (b, both[:TOK]), (b + 1, both[TOK:])

    def emit_far(u, dk, dv):
        for b, part in blocks_of(u, dk, dv):
            far_out[b] = part.astype(BF16)
            direct = jnp.logical_not(relayed(b))
            pl.when(direct)(far(b).start)
            pl.when(relayed(b))(bend_in(b).start)

    def emit_near(u, dk, dv):
        for b, part in blocks_of(u, dk, dv):
            near_out[b] = part.astype(BF16)
            near(b).start()

    def pass_row(b, part):
        two = (x < last_row - 1) & wanted(b)

        @pl.when(two)
        def _():
            near(b).wait_recv()
            far(b).wait_recv()
            row_out[b] = (part + near_in[b].astype(F32) + far_in[b].astype(F32)).astype(BF16)

        @pl.when((x < last_row) & jnp.logical_not(two))
        def _():
            near(b).wait_recv()
            row_out[b] = (part + near_in[b].astype(F32)).astype(BF16)

        @pl.when(x == last_row)
        def _():
            row_out[b] = part.astype(BF16)

        @pl.when(b != z)
        def _():
            row_copy(ring(b, -z, ROW), b).start()

        @pl.when(b == z)
        def _():
            row_in[z] = row_out[b]

    def emit_row(u, dk, dv):
        for b, part in blocks_of(u, dk, dv):
            pass_row(b, part)

    @pl.when(x >= 2)
    def _():
        whole_backward(2, near_first, emit_far)
        edge_backward(0, emit_far)
        edge_backward(1, emit_far)

    @pl.when(x >= 1)
    def _():
        whole_backward(near_first, here_first, emit_near)

    @pl.loop(QUAD, ROW)
    def _(b):
        @pl.when(relays & relayed(b))
        def _():
            bend_in(b).wait_recv()
            bend_out(b).start()

    whole_backward(here_first, 8, emit_row)
    edge_backward(8, emit_row)
    edge_backward(9, emit_row)

    for j in range(QUAD):
        cols = slice(j * TQ, (j + 1) * TQ)
        og_ref[cols, DIM:] = (dq_t[:, cols] * SCALE).T.astype(BF16)
    for d in range(QUAD):
        result_copy(1, d, spot, ring(spot, d, QUAD)).start()

    @pl.when(half == 0)
    def _():
        @pl.loop(QUAD, ROW)
        def _(b):
            pass_row(b, jnp.zeros((TOK, 2 * DIM), F32))

    collect("ctx", after_ref, relink_s, relink_r)
    write_part = maps[:, :, :DIM].reshape(length, DIM)
    for h in range(heads):
        cols = cols_of(h)
        t = tail[:, h : h + 1]
        after = head_state(after_ref, h, heads)
        input_grad_ref[:, cols] = (input_ref[:, cols] + t * dot(write, after)).astype(BF16)
        write_part += dot_nt((x_ref[:, cols].astype(F32) * t).astype(BF16), after)

    maps[:, :, :DIM] = write_part.reshape(crew, share, DIM)
    maps_in[head] = maps[head]
    scatter("head", maps, maps_in, map_s, map_r)

    collect("head", maps_in, map_s, map_r)
    added = maps_in[0]
    for i in range(1, crew):
        added += maps_in[i]
    maps_sum[...] = added.astype(BF16)
    maps_all[head] = maps_sum[...]
    spread("head", maps_sum, maps_all, all_s, all_r)

    for d in range(1, ROW):
        z_from = ring(z, -d, ROW)
        send(row_out.at[z], row_in.at[z_from], row_s.at[d], row_r.at[d], ctx=x * ROW + z_from).wait_recv()
    for a in range(QUAD):
        both = row_in[a].astype(F32) + row_in[QUAD + a].astype(F32)
        key_grad_ref[:, cols_of(a)] = both[:, :DIM].astype(BF16)
        value_grad_ref[:, cols_of(a)] = both[:, DIM:].astype(BF16)

    collect("head", maps_all, all_s, all_r)
    both = maps_all[...].reshape(length, 2 * DIM)
    write_grad_ref[...] = both[:, :DIM]
    read_grad_ref[...] = both[:, DIM:]

    for i in range(2):
        for d in range(QUAD):
            copy = result_copy(i, d, ring(spot, -d, QUAD), spot)
            if d == 0:
                copy.wait()
            else:
                copy.wait_recv()

    for d in range(1, ROW):
        for copy in key_copies(d, z, ring(z, d, ROW)):
            copy.wait_send()
        row_copy(d, ring(z, d, ROW)).wait_send()
    for d in range(1, QUAD):
        for copy in query_copies(d, spot, ring(spot, d, QUAD)):
            copy.wait_send()
        for i in range(2):
            result_copy(i, d, spot, ring(spot, d, QUAD)).wait_send()

    @pl.loop(0, ROW)
    def _(b):
        direct = wanted(b) & jnp.logical_not(relayed(b))

        @pl.when(x < last_row)
        def _():
            one_on(b).wait_send()

        @pl.when((x < last_row - 1) & direct)
        def _():
            two_on(b).wait_send()

        @pl.when((x < last_row - 1) & relayed(b))
        def _():
            turn_in(b).wait_send()

        @pl.when(relays & relayed(b))
        def _():
            turn_out(b).wait_send()
            bend_out(b).wait_send()

        @pl.when((x >= 2) & direct)
        def _():
            far(b).wait_send()

        @pl.when((x >= 2) & relayed(b))
        def _():
            bend_in(b).wait_send()

        @pl.when(x >= 1)
        def _():
            near(b).wait_send()

    settle("ctx", fact, fact_s, fact_r)
    settle("ctx", parts_out.at[0], part_s, part_r)
    settle("ctx", linked.at[0], link_s, link_r)
    settle("ctx", back_out.at[0], back_s, back_r)
    settle("ctx", relinked.at[0], relink_s, relink_r)
    settle("head", sums_out, sum_s, sum_r)
    settle("head", maps.at[0], map_s, map_r)
    settle("head", maps_sum, all_s, all_r)


def deliver_kernel(*refs):
    n = len(refs) // 2
    for src, dst in zip(refs[:n], refs[n:]):
        dst[...] = src[...]


def body(
    ssm_input,
    gate_input,
    write_map,
    read_map,
    log_decay,
    doc_start,
    ssm_grad,
    att_queries,
    att_keys,
    att_values,
    att_grad,
):
    ctx, crew = lax.axis_size("ctx"), lax.axis_size("head")
    length, width = ssm_input.shape
    heads = width // DIM
    flat, tall, attended = (length, width), (length, DIM), att_queries.shape
    part = (ctx, heads * DIM // ctx, DIM)
    block = (ROW, TOK, 2 * DIM)
    share = (crew, length // crew, 2 * DIM)
    outs = [shape(s, BF16) for s in (flat, attended, flat, flat, tall, tall, attended, attended, attended)]
    vmem, stay = pl.BlockSpec(memory_space=pltpu.VMEM), pl.BlockSpec(memory_space=pl.ANY)
    scratch = [
        ((3 * SPAN, 2 * DIM), BF16), ((QUAD, TOK, 2 * DIM), BF16), ((QUERIES, 2 * DIM), BF16), ((QUERIES, 2 * DIM), BF16),
        ((ctx, 8, DIM), F32), ((ctx, DIM), F32), ((8, DIM), F32), (tall, F32), (tall[::-1], F32), (flat, F32), (flat, BF16), (flat, F32),
        *[(part, BF16)] * 8,
        ((8, length), F32), ((crew, 8, length), F32), (share, F32), (share, F32), (share[1:], BF16), (share, BF16),
        *[(block, BF16)] * 2, ((QUAD, TOK, 2 * DIM), BF16), *[(block, BF16)] * 4,
        ((DIM, QUERIES), BF16), ((DIM, QUERIES), BF16), ((8, QUERIES), F32), ((8, QUERIES), jnp.int32),
        ((DIM, QUERIES), F32), ((DIM, QUERIES), F32), ((TK, QUERIES), BF16), ((TK, QUERIES), BF16),
    ]
    sems = [(ROW, 2)] * 2 + [(QUAD, 2)] * 2 + [(ROW,)] * 6 + [(QUAD, 2)] * 2 + [(ROW,)] * 8
    sems += [(ctx,)] * 10 + [(crew,)] * 6
    found = pl.pallas_call(
        functools.partial(mixer_kernel, width * crew),
        out_shape=tuple(outs),
        in_specs=[vmem] * 7 + [stay] * 4,
        out_specs=(vmem,) * len(outs),
        scratch_shapes=[pltpu.VMEM(s, t) for s, t in scratch] + [pltpu.SemaphoreType.DMA(s) for s in sems],
        compiler_params=pltpu.CompilerParams(
            collective_id=0, has_side_effects=True, vmem_limit_bytes=VMEM_LIMIT
        ),
    )(
        doc_start.reshape(2, length // 2), log_decay.T, ssm_input, gate_input, ssm_grad, write_map, read_map,
        att_queries, att_keys, att_values, att_grad,
    )
    return pl.pallas_call(
        deliver_kernel,
        out_shape=tuple(outs),
        in_specs=[vmem] * len(outs),
        out_specs=(vmem,) * len(outs),
    )(*found)


def solution(mesh):
    tokens, both = P("ctx", None), P("ctx", "head")
    in_specs = (both, both, tokens, tokens, both, P("ctx"), both, both, both, both, both)
    out_specs = (both, both, both, both, tokens, tokens, both, both, both)
    return jax.shard_map(body, mesh=mesh, in_specs=in_specs, out_specs=out_specs, check_vma=False)
```

```python
import functools
import math

import jax
import jax.numpy as jnp
from jax import lax
from jax.experimental import pallas as pl
from jax.experimental.pallas import tpu as pltpu
from jax.sharding import PartitionSpec as P

DIM = 128
WINDOW = 4096
EPSILON = 1e-05
ROW = 8
QUAD = 4
TQ = 256
TK = 512
QUERIES = QUAD * 256
HIDDEN = -1e30
F32 = jnp.float32
BF16 = jnp.bfloat16
EXACT = lax.Precision.HIGHEST
SCALE = DIM**-0.5
SCALE2 = SCALE * math.log2(math.e)
VMEM_LIMIT = 60 * 2**20
MESH = pl.DeviceIdType.MESH
TOK = 256
SPAN = ROW * TOK


def dot(a, b, precision=None):
    return jnp.dot(a, b, preferred_element_type=F32, precision=precision)


def dot_nt(a, b):
    return lax.dot_general(a, b, (((1,), (1,)), ((), ())), preferred_element_type=F32)


def dot_tn(a, b):
    return lax.dot_general(a, b, (((0,), (0,)), ((), ())), preferred_element_type=F32)


def shape(dims, dtype):
    return jax.ShapeDtypeStruct(dims, dtype)


def send(src, dst, sent, arrived, **where):
    return pltpu.make_async_remote_copy(
        src_ref=src, dst_ref=dst, send_sem=sent, recv_sem=arrived, device_id=where, device_id_type=MESH
    )


def ring(at, by, size):
    return lax.rem(at + by + size, size)


def greet():
    barrier = pltpu.get_barrier_semaphore()
    ctx, head = lax.axis_size("ctx"), lax.axis_size("head")
    for axis, size in (("ctx", ctx), ("head", head)):
        if size == 1:
            continue
        me = lax.axis_index(axis)

        @pl.loop(1, size)
        def _(d):
            pl.semaphore_signal(
                barrier, inc=1, device_id={axis: ring(me, d, size)}, device_id_type=MESH
            )


def await_greetings():
    pl.semaphore_wait(pltpu.get_barrier_semaphore(), lax.axis_size("ctx") + lax.axis_size("head") - 2)


def scatter(axis, src, dst, sent, arrived):
    size, me = lax.axis_size(axis), lax.axis_index(axis)

    @pl.loop(1, size)
    def _(d):
        to = ring(me, d, size)
        send(src.at[to], dst.at[me], sent.at[d], arrived.at[d], **{axis: to}).start()


def spread(axis, src, dst, sent, arrived):
    size, me = lax.axis_size(axis), lax.axis_index(axis)

    @pl.loop(1, size)
    def _(d):
        send(src, dst.at[me], sent.at[d], arrived.at[d], **{axis: ring(me, d, size)}).start()


def collect(axis, dst, sent, arrived):
    size, me = lax.axis_size(axis), lax.axis_index(axis)

    @pl.loop(1, size)
    def _(d):
        block = dst.at[ring(me, -d, size)]
        send(block, block, sent.at[d], arrived.at[d], **{axis: ring(me, d, size)}).wait_recv()


def settle(axis, src, sent, arrived):
    size, me = lax.axis_size(axis), lax.axis_index(axis)

    @pl.loop(1, size)
    def _(d):
        send(src, src, sent.at[d], arrived.at[d], **{axis: ring(me, d, size)}).wait_send()


def column(row):
    n = row.shape[1]
    same = lax.broadcasted_iota(jnp.int32, (n, n), 0) == lax.broadcasted_iota(jnp.int32, (n, n), 1)
    return jnp.sum(jnp.where(same, row, 0.0), axis=1, keepdims=True)


def tail_decay(cum, doc):
    length = cum.shape[0]
    same = doc == doc[length - 1 : length, :]
    return jnp.where(same, jnp.exp(cum[length - 1 : length, :] - cum), 0.0)


def head_decay(cum, cum_t, seen, h):
    return jnp.exp(jnp.where(seen, cum[:, h : h + 1] - cum_t[h : h + 1, :], HIDDEN))


def visible(doc, start):
    length = doc.shape[0]
    row = lax.broadcasted_iota(jnp.int32, (length, length), 0)
    col = lax.broadcasted_iota(jnp.int32, (length, length), 1)
    return (row >= col) & ((start + col).astype(F32) >= doc)


def gate_terms(gate):
    sigma = jax.nn.sigmoid(gate)
    return sigma, gate * sigma


def cols_of(h):
    return slice(h * DIM, (h + 1) * DIM)


def head_state(buf, h, heads):
    share = buf.shape[0] // heads
    return buf[h * share : (h + 1) * share].reshape(DIM, DIM)


def put_state(buf, h, heads, value):
    share = buf.shape[0] // heads
    buf[h * share : (h + 1) * share] = value.astype(BF16).reshape(share, DIM // share, DIM)


def chain(parts, linked, factor, reverse):
    n = parts.shape[0]
    edge = n - 1 if reverse else 0
    linked[edge] = jnp.zeros(linked.shape[1:], BF16)

    def one(step, total):
        i = n - 1 - step if reverse else step
        total = total * factor[pl.ds(i, 1), :] + parts[i].astype(F32)
        linked[i - 1 if reverse else i + 1] = total.astype(BF16)
        return total

    lax.fori_loop(0, n - 1, one, jnp.zeros(parts.shape[1:], F32))


def rows_of(first, block):
    return pl.ds(pl.multiple_of(first + block * TOK, TOK), TOK)


def head_block(ref, a):
    return ref.at[:, pl.ds(pl.multiple_of(a * DIM, DIM), DIM)]


HALVES = (slice(0, DIM), slice(DIM, 2 * DIM))
NEAREST = (0, 1, 7, 2, 6, 3, 5, 4)


def mixer_kernel(
    width, doc_ref, rate_ref, x_ref, gate_ref, grad_ref, write_ref, read_ref, q_ref, k_ref, v_ref, g_ref,
    out_ref, window_ref, input_grad_ref, gate_grad_ref, write_grad_ref, read_grad_ref,
    query_grad_ref, key_grad_ref, value_grad_ref,
    kv_ref, relay_ref, qg_ref, og_ref, facts_ref, factor_ref, fact, wide, turned, mixed_ref, dmixed_ref, input_ref,
    parts_out, parts_in, linked, prior_ref, back_out, back_in, relinked, after_ref,
    sums_out, sums_in, maps, maps_in, maps_sum, maps_all,
    far_out, far_in, bend_ref, near_out, near_in, row_out, row_in,
    qt_ref, gt_ref, stat_ref, low_ref, out_t, dq_t, p_ref, ds_ref,
    kv_s, kv_r, qg_s, qg_r, one_s, one_r, two_s, two_r, turn_s, turn_r, og_s, og_r,
    far_s, far_r, bend_s, bend_r, near_s, near_r, row_s, row_r,
    fact_s, fact_r, part_s, part_r, link_s, link_r, back_s, back_r, relink_s, relink_r,
    sum_s, sum_r, map_s, map_r, all_s, all_r,
):
    ctx, crew = lax.axis_size("ctx"), lax.axis_size("head")
    me, head = lax.axis_index("ctx"), lax.axis_index("head")
    x, z = me // ROW, lax.rem(me, ROW)
    spot = lax.rem(me, QUAD)
    half = z // QUAD
    last_row = ctx // ROW - 1
    heads, length = rate_ref.shape
    start = me * length

    def key_copies(d, z_from, z_to):
        out = []
        for i, ref in enumerate((k_ref, v_ref)):
            src = head_block(ref, lax.rem(z_to, QUAD))
            dst = kv_ref.at[rows_of(2 * SPAN, z_from), HALVES[i]]
            if d == 0:
                out.append(pltpu.make_async_copy(src, dst, kv_r.at[d, i]))
            else:
                out.append(send(src, dst, kv_s.at[d, i], kv_r.at[d, i], ctx=x * ROW + z_to))
        return out

    def query_copies(d, from_, to):
        out = []
        for i, ref in enumerate((q_ref, g_ref)):
            src = head_block(ref, to)
            dst = qg_ref.at[rows_of(0, from_), HALVES[i]]
            if d == 0:
                out.append(pltpu.make_async_copy(src, dst, qg_r.at[d, i]))
            else:
                out.append(send(src, dst, qg_s.at[d, i], qg_r.at[d, i], ctx=me - spot + to))
        return out

    def row_at(by):
        return lax.rem(me + by * ROW + ctx, ctx)

    def one_on(b):
        return send(
            kv_ref.at[rows_of(2 * SPAN, b), :], kv_ref.at[rows_of(SPAN, b), :],
            one_s.at[b], one_r.at[b], ctx=row_at(1),
        )

    def two_on(b):
        return send(
            kv_ref.at[rows_of(2 * SPAN, b), :], kv_ref.at[rows_of(0, b), :],
            two_s.at[b], two_r.at[b], ctx=row_at(2),
        )

    def turn_in(b):
        return send(
            kv_ref.at[rows_of(2 * SPAN, b), :], relay_ref.at[lax.rem(b, QUAD)],
            turn_s.at[b], turn_r.at[b], ctx=row_at(-1),
        )

    def turn_out(b):
        return send(
            relay_ref.at[lax.rem(b, QUAD)], kv_ref.at[rows_of(0, b), :],
            two_s.at[b], two_r.at[b], ctx=row_at(-1),
        )

    def relayed(b):
        return (z < QUAD) & (b >= QUAD)

    relays = (x == last_row) | (x + 1 < last_row - 1)

    def result_copy(i, d, a, to):
        src = og_ref.at[rows_of(0, to), HALVES[i]]
        dst = head_block((window_ref, query_grad_ref)[i], a)
        if d == 0:
            return pltpu.make_async_copy(src, dst, og_r.at[d, i])
        return send(src, dst, og_s.at[d, i], og_r.at[d, i], ctx=me - spot + to)

    def far(b):
        return send(far_out.at[b], far_in.at[b], far_s.at[b], far_r.at[b], ctx=row_at(-2))

    def bend_in(b):
        return send(far_out.at[b], bend_ref.at[lax.rem(b, QUAD)], bend_s.at[b], bend_r.at[b], ctx=row_at(1))

    def bend_out(b):
        return send(bend_ref.at[lax.rem(b, QUAD)], far_in.at[b], far_s.at[b], far_r.at[b], ctx=row_at(1))

    def near(b):
        return send(near_out.at[b], near_in.at[b], near_s.at[b], near_r.at[b], ctx=row_at(-1))

    def row_copy(d, b):
        return send(row_out.at[b], row_in.at[z], row_s.at[d], row_r.at[d], ctx=x * ROW + b)

    def wanted(b):
        return (z < QUAD) | (b >= QUAD)

    greet()

    docs = doc_ref[...].astype(F32)
    row = lax.broadcasted_iota(jnp.int32, (length, length), 0)
    col = lax.broadcasted_iota(jnp.int32, (length, length), 1)
    cum_t = dot(rate_ref[...], (row <= col).astype(F32), EXACT)
    turned[...] = jnp.zeros_like(turned)
    turned[:heads, :] = cum_t
    cum = turned[...].T[:, :heads]
    fact[...] = jnp.zeros_like(fact)
    fact[0:2, :] = docs
    fact[2:3, :heads] = cum[length - 1 : length, :]
    facts_ref[me] = fact[...]

    doc = jnp.concatenate([column(docs[0:1, :]), column(docs[1:2, :])], axis=0)
    tail = tail_decay(cum, doc)
    enter = jnp.where(doc < start.astype(F32), jnp.exp(cum), 0.0)
    write, read = write_ref[...], read_ref[...]
    for h in range(heads):
        scaled = (x_ref[:, cols_of(h)].astype(F32) * tail[:, h : h + 1]).astype(BF16)
        put_state(parts_out, h, heads, dot_tn(write, scaled))
    parts_in[me] = parts_out[me]
    await_greetings()
    scatter("ctx", parts_out, parts_in, part_s, part_r)
    spread("ctx", fact, facts_ref, fact_s, fact_r)
    for d in NEAREST[:5]:
        for copy in key_copies(d, z, ring(z, d, ROW)):
            copy.start()

    seen = visible(doc, start)
    scores = dot_nt(read, write)
    for h in range(heads):
        mix = (head_decay(cum, cum_t, seen, h) * scores).astype(BF16)
        mixed_ref[:, cols_of(h)] = dot(mix, x_ref[:, cols_of(h)])

    collect("ctx", facts_ref, fact_s, fact_r)
    at = lax.broadcasted_iota(jnp.int32, (ctx, 1), 0)
    lane = lax.broadcasted_iota(jnp.int32, (ctx, DIM), 1)
    mine = me // (ctx // heads)
    total = jnp.sum(jnp.where(lane == mine, facts_ref[:, 2, :], 0.0), axis=1, keepdims=True)
    final = jnp.sum(jnp.where(lane == DIM - 1, facts_ref[:, 1, :], 0.0), axis=1, keepdims=True)
    factor = jnp.where(final < (at * length).astype(F32), jnp.exp(total), 0.0)
    factor_ref[...] = jnp.broadcast_to(factor, factor_ref.shape)

    collect("ctx", parts_in, part_s, part_r)
    chain(parts_in, linked, factor_ref, False)
    prior_ref[me] = linked[me]
    scatter("ctx", linked, prior_ref, link_s, link_r)
    for d in NEAREST[5:]:
        for copy in key_copies(d, z, ring(z, d, ROW)):
            copy.start()
    for d in range(QUAD):
        for copy in query_copies(d, spot, ring(spot, d, QUAD)):
            copy.start()

    def keys_arrived(d):
        b = ring(z, -d, ROW)
        for copy in key_copies(d, b, z):
            if d == 0:
                copy.wait()
            else:
                copy.wait_recv()

        @pl.when((x < last_row - 1) & relayed(b))
        def _():
            turn_in(b).start()

        @pl.when(x < last_row)
        def _():
            one_on(b).start()

        @pl.when((x < last_row - 1) & wanted(b) & jnp.logical_not(relayed(b)))
        def _():
            two_on(b).start()

    for d in NEAREST[:5]:
        keys_arrived(d)

    collect("ctx", prior_ref, link_s, link_r)
    squares = jnp.zeros((length, 1), F32)
    inner = jnp.zeros((length, 1), F32)
    for h in range(heads):
        mixed = mixed_ref[:, cols_of(h)] + enter[:, h : h + 1] * dot(read, head_state(prior_ref, h, heads))
        mixed_ref[:, cols_of(h)] = mixed
        gated = mixed * gate_terms(gate_ref[:, cols_of(h)].astype(F32))[1]
        squares += jnp.sum(gated * gated, axis=1, keepdims=True)
        inner += jnp.sum(grad_ref[:, cols_of(h)].astype(F32) * gated, axis=1, keepdims=True)
    wide[...] = jnp.zeros_like(wide)
    wide[:, 0:1] = squares
    wide[:, 1:2] = inner
    sums_out[...] = wide[...].T[:8]
    sums_in[head] = sums_out[...]
    spread("head", sums_out, sums_in, sum_s, sum_r)

    for d in NEAREST[5:]:
        keys_arrived(d)

    collect("head", sums_in, sum_s, sum_r)
    sums = sums_in[0]
    for i in range(1, crew):
        sums += sums_in[i]
    sums = jnp.concatenate([sums, jnp.zeros((DIM - 8, length), F32)], axis=0).T
    rms = lax.rsqrt(sums[:, 0:1] / width + EPSILON)
    pull = rms * rms * rms * sums[:, 1:2] / width
    for h in range(heads):
        cols = cols_of(h)
        mixed = mixed_ref[:, cols]
        gate = gate_ref[:, cols].astype(F32)
        sigma, swish = gate_terms(gate)
        gated = mixed * swish
        out_ref[:, cols] = (gated * rms).astype(BF16)
        dgated = rms * grad_ref[:, cols].astype(F32) - pull * gated
        dmixed = dgated * swish
        dmixed_ref[:, cols] = dmixed.astype(BF16)
        gate_grad_ref[:, cols] = (dgated * mixed * sigma * (1.0 + gate * (1.0 - sigma))).astype(BF16)
        put_state(back_out, h, heads, dot_tn(read, (enter[:, h : h + 1] * dmixed).astype(BF16)))
    back_in[me] = back_out[me]
    scatter("ctx", back_out, back_in, back_s, back_r)

    @pl.loop(QUAD, ROW)
    def _(b):
        @pl.when(relays & relayed(b))
        def _():
            turn_in(b).wait_recv()
            turn_out(b).start()

    for d in range(QUAD):
        for copy in query_copies(d, ring(spot, -d, QUAD), spot):
            if d == 0:
                copy.wait()
            else:
                copy.wait_recv()

    first_key = half * QUERIES

    def keys_of(u):
        return pl.ds(pl.multiple_of(first_key + u * TK, TK), TK)

    def tile(j):
        return pl.ds(pl.multiple_of(j * TQ, TQ), TQ)

    for j in range(QUAD):
        cols = slice(j * TQ, (j + 1) * TQ)
        qt_ref[:, cols] = qg_ref[cols, :DIM].T
        gt_ref[:, cols] = qg_ref[cols, DIM:].T
        own = facts_ref[me - spot + j]
        own = jnp.concatenate([own[0:1, :], own[1:2, :]], axis=1).astype(jnp.int32)
        high = 2 * SPAN + first_key + j * TQ + lax.broadcasted_iota(jnp.int32, (1, TQ), 1)
        low_ref[0:1, cols] = jnp.maximum(own - (x - 2) * SPAN, high - (WINDOW - 1))
        low_ref[1:2, cols] = high
    stat_ref[0:1, :] = jnp.full((1, QUERIES), HIDDEN, F32)
    stat_ref[1:2, :] = jnp.zeros((1, QUERIES), F32)
    out_t[...] = jnp.zeros_like(out_t)
    dq_t[...] = jnp.zeros_like(dq_t)

    def score(u, j, edge):
        s = dot(kv_ref[keys_of(u), :DIM], qt_ref[:, tile(j)])
        at = first_key + u * TK + lax.broadcasted_iota(jnp.int32, (TK, TQ), 0)
        shown = at >= low_ref[0:1, tile(j)]
        if edge:
            shown = shown & (at <= low_ref[1:2, tile(j)])
        return jnp.where(shown, s, HIDDEN)

    def forward(u, j, values_t, edge):
        cols = tile(j)
        s = score(u, j, edge)
        top = stat_ref[0:1, cols]
        new = jnp.maximum(top, jnp.max(s, axis=0, keepdims=True))
        p = jnp.exp2((s - new) * SCALE2)
        keep = jnp.exp2((top - new) * SCALE2)
        stat_ref[0:1, cols] = new
        stat_ref[1:2, cols] = stat_ref[1:2, cols] * keep + jnp.sum(p, axis=0, keepdims=True)
        out_t[:, cols] = out_t[:, cols] * keep + dot(values_t, p.astype(BF16))

    def whole_forward(begin, end):
        @pl.loop(begin, end)
        def _(u):
            values_t = kv_ref[keys_of(u), DIM:].T
            for j in range(QUAD):
                forward(u, j, values_t, False)

    def tiles_of_edge(u):
        return (0, 2 * u + 2) if u < 2 else (2 * (u - 8), QUAD)

    def edge_forward(u):
        values_t = kv_ref[keys_of(u), DIM:].T

        @pl.loop(*tiles_of_edge(u))
        def _(j):
            forward(u, j, values_t, True)

    near_first, here_first = QUAD - 2 * half, 8 - 2 * half

    edge_forward(8)
    edge_forward(9)

    whole_forward(here_first, 8)

    @pl.when(x >= 1)
    def _():
        @pl.loop(0, ROW)
        def _(b):
            one_on(b).wait_recv()

        whole_forward(near_first, here_first)

    collect("ctx", back_in, back_s, back_r)
    chain(back_in, relinked, factor_ref, True)
    after_ref[me] = relinked[me]
    scatter("ctx", relinked, after_ref, relink_s, relink_r)

    @pl.when(x >= 2)
    def _():
        @pl.loop(0, ROW)
        def _(b):
            @pl.when(wanted(b))
            def _():
                two_on(b).wait_recv()

        whole_forward(2, near_first)
        edge_forward(0)
        edge_forward(1)

    for j in range(QUAD):
        cols = slice(j * TQ, (j + 1) * TQ)
        total = stat_ref[1:2, cols]
        attended = out_t[:, cols] / total
        og_ref[cols, :DIM] = attended.T.astype(BF16)
        stat_ref[2:3, cols] = stat_ref[0:1, cols] * SCALE2 + jnp.log2(total)
        stat_ref[3:4, cols] = jnp.sum(gt_ref[:, cols].astype(F32) * attended, axis=0, keepdims=True)
    for d in range(QUAD):
        result_copy(0, d, spot, ring(spot, d, QUAD)).start()

    def backward(u, j, edge):
        cols = tile(j)
        p = jnp.exp2(score(u, j, edge) * SCALE2 - stat_ref[2:3, cols])
        dp = dot(kv_ref[keys_of(u), DIM:], gt_ref[:, cols])
        p_ref[:, cols] = p.astype(BF16)
        ds_ref[:, cols] = (p * (dp - stat_ref[3:4, cols])).astype(BF16)

    def gather_backward(u):
        dq_t[...] += dot(kv_ref[keys_of(u), :DIM].T, ds_ref[...])
        return dot(ds_ref[...], qg_ref[:, :DIM]) * SCALE, dot(p_ref[...], qg_ref[:, DIM:])

    def whole_backward(begin, end, emit):
        @pl.loop(begin, end)
        def _(u):
            for j in range(QUAD):
                backward(u, j, False)
            emit(u, *gather_backward(u))

    def edge_backward(u, emit):
        begin, end = tiles_of_edge(u)
        if end - begin < QUAD:
            p_ref[...] = jnp.zeros_like(p_ref)
            ds_ref[...] = jnp.zeros_like(ds_ref)

        @pl.loop(begin, end)
        def _(j):
            backward(u, j, True)

        emit(u, *gather_backward(u))

    def blocks_of(u, dk, dv):
        b = lax.rem(2 * u + QUAD * half, ROW)
        both = jnp.concatenate([dk, dv], axis=1)
        return (b, both[:TOK]), (b + 1, both[TOK:])

    def emit_far(u, dk, dv):
        for b, part in blocks_of(u, dk, dv):
            far_out[b] = part.astype(BF16)
            direct = jnp.logical_not(relayed(b))
            pl.when(direct)(far(b).start)
            pl.when(relayed(b))(bend_in(b).start)

    def emit_near(u, dk, dv):
        for b, part in blocks_of(u, dk, dv):
            near_out[b] = part.astype(BF16)
            near(b).start()

    def pass_row(b, part):
        two = (x < last_row - 1) & wanted(b)

        @pl.when(two)
        def _():
            near(b).wait_recv()
            far(b).wait_recv()
            row_out[b] = (part + near_in[b].astype(F32) + far_in[b].astype(F32)).astype(BF16)

        @pl.when((x < last_row) & jnp.logical_not(two))
        def _():
            near(b).wait_recv()
            row_out[b] = (part + near_in[b].astype(F32)).astype(BF16)

        @pl.when(x == last_row)
        def _():
            row_out[b] = part.astype(BF16)

        @pl.when(b != z)
        def _():
            row_copy(ring(b, -z, ROW), b).start()

        @pl.when(b == z)
        def _():
            row_in[z] = row_out[b]

    def emit_row(u, dk, dv):
        for b, part in blocks_of(u, dk, dv):
            pass_row(b, part)

    @pl.when(x >= 2)
    def _():
        whole_backward(2, near_first, emit_far)
        edge_backward(0, emit_far)
        edge_backward(1, emit_far)

    @pl.when(x >= 1)
    def _():
        whole_backward(near_first, here_first, emit_near)

    @pl.loop(QUAD, ROW)
    def _(b):
        @pl.when(relays & relayed(b))
        def _():
            bend_in(b).wait_recv()
            bend_out(b).start()

    whole_backward(here_first, 8, emit_row)
    edge_backward(8, emit_row)
    edge_backward(9, emit_row)

    for j in range(QUAD):
        cols = slice(j * TQ, (j + 1) * TQ)
        og_ref[cols, DIM:] = (dq_t[:, cols] * SCALE).T.astype(BF16)
    for d in range(QUAD):
        result_copy(1, d, spot, ring(spot, d, QUAD)).start()

    @pl.when(half == 0)
    def _():
        @pl.loop(QUAD, ROW)
        def _(b):
            pass_row(b, jnp.zeros((TOK, 2 * DIM), F32))

    pairs = jnp.zeros_like(scores)
    read_part = jnp.zeros(read.shape, F32)
    for h in range(heads):
        cols = cols_of(h)
        decay = head_decay(cum, cum_t, seen, h)
        dmixed = dmixed_ref[:, cols]
        input_ref[:, cols] = dot_tn((decay * scores).astype(BF16), dmixed)
        pairs += decay * dot_nt(dmixed, x_ref[:, cols])
        entered = (enter[:, h : h + 1] * dmixed.astype(F32)).astype(BF16)
        read_part += dot_nt(entered, head_state(prior_ref, h, heads))
    pairs = pairs.astype(BF16)
    share = length // crew
    maps[:, :, :DIM] = dot_tn(pairs, read).reshape(crew, share, DIM)
    maps[:, :, DIM:] = (read_part + dot(pairs, write)).reshape(crew, share, DIM)

    collect("ctx", after_ref, relink_s, relink_r)
    write_part = maps[:, :, :DIM].reshape(length, DIM)
    for h in range(heads):
        cols = cols_of(h)
        t = tail[:, h : h + 1]
        after = head_state(after_ref, h, heads)
        input_grad_ref[:, cols] = (input_ref[:, cols] + t * dot(write, after)).astype(BF16)
        write_part += dot_nt((x_ref[:, cols].astype(F32) * t).astype(BF16), after)

    maps[:, :, :DIM] = write_part.reshape(crew, share, DIM)
    maps_in[head] = maps[head]
    scatter("head", maps, maps_in, map_s, map_r)

    collect("head", maps_in, map_s, map_r)
    added = maps_in[0]
    for i in range(1, crew):
        added += maps_in[i]
    maps_sum[...] = added.astype(BF16)
    maps_all[head] = maps_sum[...]
    spread("head", maps_sum, maps_all, all_s, all_r)

    for d in range(1, ROW):
        z_from = ring(z, -d, ROW)
        send(row_out.at[z], row_in.at[z_from], row_s.at[d], row_r.at[d], ctx=x * ROW + z_from).wait_recv()
    for a in range(QUAD):
        both = row_in[a].astype(F32) + row_in[QUAD + a].astype(F32)
        key_grad_ref[:, cols_of(a)] = both[:, :DIM].astype(BF16)
        value_grad_ref[:, cols_of(a)] = both[:, DIM:].astype(BF16)

    collect("head", maps_all, all_s, all_r)
    both = maps_all[...].reshape(length, 2 * DIM)
    write_grad_ref[...] = both[:, :DIM]
    read_grad_ref[...] = both[:, DIM:]

    for i in range(2):
        for d in range(QUAD):
            copy = result_copy(i, d, ring(spot, -d, QUAD), spot)
            if d == 0:
                copy.wait()
            else:
                copy.wait_recv()

    for d in range(1, ROW):
        for copy in key_copies(d, z, ring(z, d, ROW)):
            copy.wait_send()
        row_copy(d, ring(z, d, ROW)).wait_send()
    for d in range(1, QUAD):
        for copy in query_copies(d, spot, ring(spot, d, QUAD)):
            copy.wait_send()
        for i in range(2):
            result_copy(i, d, spot, ring(spot, d, QUAD)).wait_send()

    @pl.loop(0, ROW)
    def _(b):
        direct = wanted(b) & jnp.logical_not(relayed(b))

        @pl.when(x < last_row)
        def _():
            one_on(b).wait_send()

        @pl.when((x < last_row - 1) & direct)
        def _():
            two_on(b).wait_send()

        @pl.when((x < last_row - 1) & relayed(b))
        def _():
            turn_in(b).wait_send()

        @pl.when(relays & relayed(b))
        def _():
            turn_out(b).wait_send()
            bend_out(b).wait_send()

        @pl.when((x >= 2) & direct)
        def _():
            far(b).wait_send()

        @pl.when((x >= 2) & relayed(b))
        def _():
            bend_in(b).wait_send()

        @pl.when(x >= 1)
        def _():
            near(b).wait_send()

    settle("ctx", fact, fact_s, fact_r)
    settle("ctx", parts_out.at[0], part_s, part_r)
    settle("ctx", linked.at[0], link_s, link_r)
    settle("ctx", back_out.at[0], back_s, back_r)
    settle("ctx", relinked.at[0], relink_s, relink_r)
    settle("head", sums_out, sum_s, sum_r)
    settle("head", maps.at[0], map_s, map_r)
    settle("head", maps_sum, all_s, all_r)


def deliver_kernel(*refs):
    n = len(refs) // 2
    for src, dst in zip(refs[:n], refs[n:]):
        dst[...] = src[...]


def body(
    ssm_input,
    gate_input,
    write_map,
    read_map,
    log_decay,
    doc_start,
    ssm_grad,
    att_queries,
    att_keys,
    att_values,
    att_grad,
):
    ctx, crew = lax.axis_size("ctx"), lax.axis_size("head")
    length, width = ssm_input.shape
    heads = width // DIM
    flat, tall, attended = (length, width), (length, DIM), att_queries.shape
    part = (ctx, heads * DIM // ctx, DIM)
    block = (ROW, TOK, 2 * DIM)
    share = (crew, length // crew, 2 * DIM)
    outs = [shape(s, BF16) for s in (flat, attended, flat, flat, tall, tall, attended, attended, attended)]
    vmem, stay = pl.BlockSpec(memory_space=pltpu.VMEM), pl.BlockSpec(memory_space=pl.ANY)
    scratch = [
        ((3 * SPAN, 2 * DIM), BF16), ((QUAD, TOK, 2 * DIM), BF16), ((QUERIES, 2 * DIM), BF16), ((QUERIES, 2 * DIM), BF16),
        ((ctx, 8, DIM), F32), ((ctx, DIM), F32), ((8, DIM), F32), (tall, F32), (tall[::-1], F32), (flat, F32), (flat, BF16), (flat, F32),
        *[(part, BF16)] * 8,
        ((8, length), F32), ((crew, 8, length), F32), (share, F32), (share, F32), (share[1:], BF16), (share, BF16),
        *[(block, BF16)] * 2, ((QUAD, TOK, 2 * DIM), BF16), *[(block, BF16)] * 4,
        ((DIM, QUERIES), BF16), ((DIM, QUERIES), BF16), ((8, QUERIES), F32), ((8, QUERIES), jnp.int32),
        ((DIM, QUERIES), F32), ((DIM, QUERIES), F32), ((TK, QUERIES), BF16), ((TK, QUERIES), BF16),
    ]
    sems = [(ROW, 2)] * 2 + [(QUAD, 2)] * 2 + [(ROW,)] * 6 + [(QUAD, 2)] * 2 + [(ROW,)] * 8
    sems += [(ctx,)] * 10 + [(crew,)] * 6
    found = pl.pallas_call(
        functools.partial(mixer_kernel, width * crew),
        out_shape=tuple(outs),
        in_specs=[vmem] * 7 + [stay] * 4,
        out_specs=(vmem,) * len(outs),
        scratch_shapes=[pltpu.VMEM(s, t) for s, t in scratch] + [pltpu.SemaphoreType.DMA(s) for s in sems],
        compiler_params=pltpu.CompilerParams(
            collective_id=0, has_side_effects=True, vmem_limit_bytes=VMEM_LIMIT
        ),
    )(
        doc_start.reshape(2, length // 2), log_decay.T, ssm_input, gate_input, ssm_grad, write_map, read_map,
        att_queries, att_keys, att_values, att_grad,
    )
    return pl.pallas_call(
        deliver_kernel,
        out_shape=tuple(outs),
        in_specs=[vmem] * len(outs),
        out_specs=(vmem,) * len(outs),
    )(*found)


def solution(mesh):
    tokens, both = P("ctx", None), P("ctx", "head")
    in_specs = (both, both, tokens, tokens, both, P("ctx"), both, both, both, both, both)
    out_specs = (both, both, both, both, tokens, tokens, both, both, both)
    return jax.shard_map(body, mesh=mesh, in_specs=in_specs, out_specs=out_specs, check_vma=False)
```
